32 devices in a mesh: users: 2 (over x), ctx: 4 (over z), head: 4 (over y, core).
Axes of the slice: x: 2, y: 2, z: 4, core: 2. Of those that a mesh axis runs over, the one named last changes fastest.
Arguments:
- counts: int32 [2], P('users'), may hold values from 64 to 512, as said below
- cand_owner: int32 [2, 512, 1], P('users', 'ctx'), may hold values from 0 to 7; in each aligned block of 128 rows (0 to 127, 128 to 255, ..., all dimensions but the last counted through in order) at most 32 rows name the same one
- cand_row: int32 [2, 512], P('users', 'ctx'), may hold values from 0 to 127
- item_table: bfloat16 [1024, 1024], P(('users', 'ctx')), may hold values from -6 to 6
- proj_weight: bfloat16 [1024, 4, 1024], P(None, None, 'head'), may hold values from -0.1875 to 0.1875
- out_weight: bfloat16 [1024, 1024], P('head'), may hold values from -0.1875 to 0.1875
- key_cache: bfloat16 [2, 2048, 1024], P('users', 'ctx', 'head'), may hold values from -6 to 6
- value_cache: bfloat16 [2, 2048, 1024], P('users', 'ctx', 'head'), may hold values from -6 to 6
Outputs:
- mixed: bfloat16 [2, 512, 1024], P('users', 'ctx', 'head')
The draws below stay inside these ranges and needn't reach their ends.
Inputs may be any that keep to these rules, and one draw needn't show every extreme that they name: `counts`: some user has all 512 slots live. `cand_owner`: among the 128 slots of one user on one index of ctx, at most 32 name the same owner, a bound that some block reaches.
All inputs are finite; a program needn't handle non-finite values.
Results may differ from the reference program's by a relative error of at most 0.0056.
Values may be sent and summed in bfloat16 or wider, within the bound.
No kernel may reach another device: no remote copies, remote signals or barrier semaphores. Data moves between devices by JAX's collectives and lax.ppermute only.
A program may use at most 64 MiB of HBM per device.

```python
import math
import jax
import jax.numpy as jnp
import numpy as np
from jax import lax

D = 1024
HEADS = 8
HEAD_DIM = 128
CSLOT = 128
ITEM_DEV = 128
HD = 1024
USERS = 2
HIST = 2048
CAND = 512
NOWN = 8
ITEMS = 1024
CAP = 32


def draw_counts(key, part):
    first_key = jax.random.fold_in(key, 11)
    second_key = jax.random.fold_in(key, 23)
    drawn = jax.random.randint(first_key, (USERS,), CAND // 8, CAND + 1)
    fullest = jax.random.randint(second_key, (), 0, USERS)
    return jnp.where(jnp.arange(USERS) == fullest, CAND, drawn).astype(jnp.int32)


def set_ends(result, rng, smallest, largest):
    dims = result.shape
    place = [jax.random.randint(jax.random.fold_in(rng, axis), (), 0, dims[axis]) for axis in range(len(dims))]
    result = result.at[tuple(place)].set(smallest)
    longest = dims.index(max(dims))
    place[longest] = (place[longest] + 1) % dims[longest]
    return result.at[tuple(place)].set(largest)


def level_of(key, dims, cuts, low, top_value):
    level = 1.0
    for axis_at, shards_of in cuts:
        draws = jax.random.uniform(jax.random.fold_in(jax.random.fold_in(key, 6), axis_at), (shards_of,), jnp.float32, low / len(cuts), top_value / len(cuts))
        level = level * jnp.repeat(jnp.exp(draws), dims[axis_at] // shards_of).reshape((-1,) + (1,) * (len(dims) - 1 - axis_at))
    return level


def routed_block(own_key, own, number, rows, number_of, top, reach, skew):
    order = jax.random.permutation(own_key, number_of)
    crowded, common = portions_of(number_of, rows * top, reach, skew, True), portions_of(number_of, rows * top, reach, skew, False)
    places = jnp.arange(number_of)

    def named(tallies, offset_by):
        used = int((tallies > 0).sum())
        fixed = max(1, used // 4)
        moved = fixed + (places - fixed + offset_by * (used - fixed)) % max(1, number_of - fixed)
        return jnp.zeros((number_of,), jnp.int32).at[order[jnp.where(places < fixed, places, moved)]].set(jnp.asarray(tallies, jnp.int32))

    tallies = jnp.where(number % 4 == 0, named(crowded, number // 4), named(common, number - number // 4 - 1))
    mixed = jax.random.permutation(jax.random.fold_in(own, 3), number_of)
    source_of, receiver = mixed[0:number_of // 2 * 2:2], mixed[1:number_of // 2 * 2:2]
    room = jnp.minimum(tallies[source_of] - 1, reach - tallies[receiver]) // 2
    room = jnp.where((source_of == order[0]) | (receiver == order[0]) | (tallies[receiver] == 0), 0, jnp.maximum(room, 0))
    moved = jax.random.randint(jax.random.fold_in(own, 4), (number_of // 2,), 0, 1 << 20) % (room + 1)
    tallies = tallies.at[source_of].add(-moved).at[receiver].add(moved)
    labels = jnp.searchsorted(jnp.cumsum(tallies), jnp.arange(rows * top), side="right").astype(jnp.int32)
    grid = labels.reshape(top, rows).T
    grid = grid[jax.random.permutation(jax.random.fold_in(own, 1), rows)]
    offset_by = jax.random.randint(jax.random.fold_in(own, 2), (rows, 1), 0, top)
    return jnp.take_along_axis(grid, (jnp.arange(top)[None, :] + offset_by) % top, axis=1)


def portions_of(amount, total, reach, slope, full):
    loads = [(1 << 20) // math.isqrt(rank ** slope) + 1 for rank in range(1, amount + 1)]
    largest = reach if full else min(reach, max(-(-total // amount), total * loads[0] // sum(loads)))
    least = 1 if total - largest >= amount - 1 else 0
    given, rest = [largest] + [least] * (amount - 1), total - largest - least * (amount - 1)
    while rest > 0:
        free = [i for i in range(1, amount) if given[i] < largest] or [i for i in range(1, amount) if given[i] < reach]
        whole, left = sum([loads[i] for i in free]), rest
        for i in free:
            extra = min(reach - given[i], max(1, left * loads[i] // whole), rest)
            given[i] = given[i] + extra
            rest = rest - extra
    return np.array(given)


def scatter_about(rng, extent, deviation, reach, pieces=(), kind=jnp.bfloat16):
    gain = level_of(rng, extent, pieces, -0.22, 0.18) if pieces else 1.0
    result = jax.random.normal(rng, extent, jnp.float32) * deviation * gain
    return jnp.minimum(jnp.maximum(result, -reach), reach).astype(kind)


def setup_inputs(seed: int = 0) -> dict:
    key_of = jax.random.split(jax.random.key(seed), 9)
    counts = draw_counts(jax.random.fold_in(key_of[8], 71), 0)
    cand_owner_keys = jax.random.split(jax.random.fold_in(key_of[1], 1), USERS * CAND // CSLOT)
    cand_owner_turns = jax.random.permutation(jax.random.fold_in(key_of[1], 3), USERS * CAND // CSLOT)
    cand_owner = jax.vmap(lambda own, number: routed_block(jax.random.fold_in(key_of[1], 2), own, number, CSLOT, NOWN, 1, CAP, 1))(cand_owner_keys, cand_owner_turns).reshape((USERS, CAND, 1))
    cand_row = set_ends(jax.random.randint(key_of[2], (USERS, CAND), 0, ITEM_DEV), jax.random.fold_in(key_of[2], 1), 0, ITEM_DEV - 1).astype(jnp.int32)
    item_table = scatter_about(key_of[3], (ITEMS, D), 1.0, 6.0, ((0, 8),))
    proj_weight = scatter_about(key_of[4], (D, 4, HD), D ** -0.5, 0.1875, ((2, 4),))
    out_weight = scatter_about(key_of[5], (HD, D), HD ** -0.5, 0.1875, ((0, 4),))
    key_cache = scatter_about(key_of[6], (USERS, HIST, HD), 1.0, 6.0, ((0, 2), (1, 4), (2, 4)))
    value_cache = scatter_about(key_of[7], (USERS, HIST, HD), 1.0, 6.0, ((0, 2), (1, 4), (2, 4)))
    return dict(counts=counts, cand_owner=cand_owner, cand_row=cand_row, item_table=item_table, proj_weight=proj_weight, out_weight=out_weight, key_cache=key_cache, value_cache=value_cache)


def attend_rows(query_block, keys_full, values_full):
    rows_here = query_block.shape[0]
    query_heads = query_block.reshape(rows_here, HEADS, HEAD_DIM)
    scores = jnp.einsum('bhd,nhd->hbn', query_heads, keys_full, precision=lax.Precision.HIGHEST) * HEAD_DIM ** (-0.5)
    weights = jax.nn.silu(scores).astype(jnp.bfloat16).astype(jnp.float32)
    summed = jnp.einsum('hbn,nhd->bhd', weights, values_full, precision=lax.Precision.HIGHEST)
    return summed.reshape(rows_here, HD)

def one_user(packed, item_table, proj_weight, out_weight):
    user_count, owner, local_rows, keys, values = packed
    item_ids = (owner[:, 0] * ITEM_DEV + local_rows).astype(jnp.int32)
    embedded = jnp.take(item_table, item_ids, axis=0)
    values_in = embedded.astype(jnp.float32)
    center = values_in - lax.optimization_barrier(jnp.mean(values_in, axis=1, keepdims=True))
    normed = (center * lax.rsqrt(lax.optimization_barrier(jnp.mean(center * center, axis=1, keepdims=True)) + 1e-05)).astype(jnp.bfloat16)
    projected = jnp.dot(normed, proj_weight.reshape(D, 4 * HD), preferred_element_type=jnp.float32)
    acts = jax.nn.silu(projected).astype(jnp.bfloat16).reshape(CAND, 4, HD)
    gates_all = acts[:, 0].astype(jnp.float32)
    values_all = acts[:, 1].astype(jnp.float32)
    queries_all = acts[:, 2].astype(jnp.float32)
    keys_all = acts[:, 3].astype(jnp.float32)
    keys_full = keys.astype(jnp.float32).reshape(HIST, HEADS, HEAD_DIM)
    values_full = values.astype(jnp.float32).reshape(HIST, HEADS, HEAD_DIM)
    block = math.gcd(CAND, 512)
    query_blocks = queries_all.reshape(CAND // block, block, HD)
    cache_term = lax.map(lambda query_block: attend_rows(query_block, keys_full, values_full), query_blocks).reshape(CAND, HEADS, HEAD_DIM)
    own_scores = lax.optimization_barrier(jnp.sum((queries_all * keys_all).reshape(CAND, HEADS, HEAD_DIM), axis=2)) * HEAD_DIM ** (-0.5)
    own_weight = jax.nn.silu(own_scores)
    attended = cache_term * HIST ** (-0.5) + own_weight[:, :, None] * values_all.reshape(CAND, HEADS, HEAD_DIM)
    head_center = attended - lax.optimization_barrier(jnp.mean(attended, axis=2, keepdims=True))
    head_normed = head_center * lax.rsqrt(lax.optimization_barrier(jnp.mean(head_center * head_center, axis=2, keepdims=True)) + 1e-05)
    hidden = (head_normed.reshape(CAND, HD) * gates_all).astype(jnp.bfloat16)
    projected_out = jnp.dot(hidden, out_weight, preferred_element_type=jnp.float32)
    live = (jnp.arange(CAND, dtype=jnp.int32) < user_count)[:, None]
    return jnp.where(live, values_in + projected_out, 0.0).astype(jnp.bfloat16)

def reference(counts, cand_owner, cand_row, item_table, proj_weight, out_weight, key_cache, value_cache):
    return lax.map(lambda packed: one_user(packed, item_table, proj_weight, out_weight), (counts, cand_owner, cand_row, key_cache, value_cache))
```

```python
import jax
import jax.numpy as jnp
from jax import lax
from jax.experimental import pallas as pl
from jax.experimental.pallas import tpu as pltpu
from jax.sharding import PartitionSpec as P

HEAD_DIM = 128
PAD = 16
F32 = jnp.float32
BF16 = jnp.bfloat16


def silu(v):
    return 0.5 * v * (1.0 + jnp.tanh(0.5 * v))


def dot(a, b):
    return jnp.dot(a, b, preferred_element_type=F32)


def vmem():
    return pl.BlockSpec(memory_space=pltpu.VMEM)


def call(kernel, outs, scratch=(), name=None):
    return pl.pallas_call(
        kernel,
        out_shape=outs,
        out_specs=jax.tree.map(lambda _: vmem(), outs),
        scratch_shapes=list(scratch),
        name=name,
    )


def shape(dims, kind=BF16):
    return jax.ShapeDtypeStruct(dims, kind)


def queries_kernel(owner_ref, row_ref, table_ref, weight_ref, packet_ref, normed_ref):
    rows = table_ref.shape[0]
    x = table_ref[...].astype(F32)
    center = x - jnp.mean(x, axis=1, keepdims=True)
    normed = (center * lax.rsqrt(jnp.mean(center * center, axis=1, keepdims=True) + 1e-05)).astype(BF16)
    normed_ref[...] = normed
    packet_ref[0:rows, :] = silu(dot(normed, weight_ref[...])).astype(BF16)
    slots = owner_ref.shape[1]
    packet_ref[rows:, 0:slots] = jnp.broadcast_to(owner_ref[...].astype(F32), (PAD, slots)).astype(BF16)
    packet_ref[rows:, slots : 2 * slots] = jnp.broadcast_to(row_ref[...].astype(F32), (PAD, slots)).astype(BF16)


def rest_kernel(normed_ref, weight_ref, packet_ref, table_ref, bulk_ref):
    rows = normed_ref.shape[0]
    width = packet_ref.shape[1]
    normed = normed_ref[...]
    gates = silu(dot(normed, weight_ref[:, 0:width])).astype(BF16)
    values = silu(dot(normed, weight_ref[:, width : 2 * width])).astype(BF16).astype(F32)
    keys = silu(dot(normed, weight_ref[:, 3 * width :])).astype(BF16).astype(F32)
    for first in range(0, width, HEAD_DIM):
        cols = slice(first, first + HEAD_DIM)
        score = jnp.sum(packet_ref[0:rows, cols].astype(F32) * keys[:, cols], axis=1, keepdims=True)
        bulk_ref[:, cols] = (silu(score * HEAD_DIM ** (-0.5)) * values[:, cols]).astype(BF16)
    bulk_ref[:, width : 2 * width] = gates
    start = pl.multiple_of(lax.axis_index("head") * width, width)
    bulk_ref[:, 2 * width :] = table_ref[:, pl.ds(start, width)]


def attend_kernel(users, group_size, held, history, *refs):
    groups = refs[:group_size]
    bulks = refs[group_size : group_size + users]
    key_ref, value_ref = refs[group_size + users : group_size + users + 2]
    packet_ref, mine_ref, query_ref, id_ref, sum_ref = refs[group_size + users + 2 :]
    me_user = lax.axis_index("users")
    me_ctx = lax.axis_index("ctx")
    ctx_size = group_size
    rows = bulks[0].shape[0]
    span = rows + PAD
    width = key_ref.shape[1]
    slots = query_ref.shape[0] // ctx_size
    owners = [[(me_user ^ k) * ctx_size + (me_ctx ^ m) for k in range(users)] for m in range(ctx_size)]
    owners = [[o.astype(F32) for o in line] for line in owners]
    for m in range(ctx_size):
        id_ref[m] = jnp.transpose(groups[m][rows:span, :].astype(F32))

    def place(j, carry):
        ids = id_ref[j]
        owner = ids[0:slots, 0:1]
        row = ids[slots : 2 * slots, 0:1]
        total = jnp.zeros((slots, width), F32)
        for m in range(ctx_size):
            spot = jnp.full((slots, 1), -1.0, F32)
            for k in range(users):
                spot = jnp.where(owner == owners[m][k], row + float(k * span), spot)
            lanes = lax.broadcasted_iota(jnp.int32, (slots, users * span), 1).astype(F32)
            total = total + dot((lanes == spot).astype(F32).astype(BF16), groups[m][...])
        first = pl.multiple_of(j * slots, slots)
        query_ref[pl.ds(first, slots), :] = total.astype(BF16)
        return carry

    lax.fori_loop(0, ctx_size, place, 0, unroll=ctx_size <= 4)
    count = ctx_size * slots
    block = min(count, 512)

    def attend(b, carry):
        first = pl.multiple_of(b * block, block)
        for at in range(0, width, HEAD_DIM):
            cols = slice(at, at + HEAD_DIM)
            scores = lax.dot_general(
                query_ref[pl.ds(first, block), cols], key_ref[:, cols],
                (((1,), (1,)), ((), ())), preferred_element_type=F32,
            ) * HEAD_DIM ** (-0.5)
            sum_ref[pl.ds(first, block), cols] = dot(silu(scores).astype(BF16), value_ref[:, cols])
        return carry

    lax.fori_loop(0, count // block, attend, 0, unroll=count // block <= 2)
    before = (
        lax.broadcasted_iota(jnp.int32, (slots, slots), 0) < lax.broadcasted_iota(jnp.int32, (slots, slots), 1)
    ).astype(F32).astype(BF16)

    def finish(j, carry):
        ids = id_ref[j]
        owner = ids[0:slots, 0:1]
        row = ids[slots : 2 * slots, 0:1]
        extra = jnp.zeros((slots, 3 * width), F32)
        lanes = lax.broadcasted_iota(jnp.int32, (slots, rows), 1).astype(F32)
        for k in range(users):
            spot = jnp.where(owner == owners[0][k], row, -1.0)
            extra = extra + dot((lanes == spot).astype(F32).astype(BF16), bulks[k][...])
        first = pl.multiple_of(j * slots, slots)
        packet_ref[j, 0:slots, :] = (
            sum_ref[pl.ds(first, slots), :] * history ** (-0.5) + extra[:, 0:width]
        ).astype(BF16)
        return extra[:, width:].astype(BF16)

    mine_ref[...] = finish(0, 0)
    if ctx_size <= 4:
        todo = range(1, ctx_size)
    else:
        todo = range(1, ctx_size)
    for j in todo:
        rest = finish(j, 0)
        owner = groups[j][rows:span, 0:slots].astype(F32)
        inside = jnp.zeros((PAD, slots), jnp.bool_)
        for k in range(users):
            inside = inside | (owner == owners[0][k])
        rank = dot(inside.astype(F32).astype(BF16), before)
        rank = jnp.where(inside, rank, -1.0)[0:1, :]
        pick = (lax.broadcasted_iota(jnp.int32, (held, slots), 0).astype(F32) == rank).astype(F32).astype(BF16)
        packed = dot(pick, rest).astype(BF16)
        packet_ref[j, slots : slots + held, :] = packed[:, 0:width]
        packet_ref[j, slots + held :, :] = packed[:, width:]


def mix_kernel(users, ctx_size, head_size, held, *refs):
    owner_ref, packet_ref, mine_ref = refs[:3]
    others = refs[3 : 3 + ctx_size - 1]
    weight_ref = refs[2 + ctx_size]
    outs = refs[3 + ctx_size : 3 + ctx_size + head_size]
    residual_ref = refs[3 + ctx_size + head_size]
    me_user = lax.axis_index("users")
    me_ctx = lax.axis_index("ctx")
    me_head = lax.axis_index("head")
    slots, width = mine_ref.shape[0], mine_ref.shape[1] // 2
    owner = jnp.transpose(jnp.broadcast_to(owner_ref[...].astype(F32), (8, slots)))[:, 0:1]
    lanes = 128
    lane = lax.broadcasted_iota(jnp.int32, (slots, lanes), 1)
    inside = jnp.zeros((slots, lanes), jnp.bool_)
    for k in range(users):
        named = (me_user ^ k) * ctx_size + (me_ctx ^ lane)
        inside = inside | ((owner == named.astype(F32)) & (lane < ctx_size))
    after = (
        lax.broadcasted_iota(jnp.int32, (slots, slots), 1) < lax.broadcasted_iota(jnp.int32, (slots, slots), 0)
    ).astype(F32).astype(BF16)
    rank = jnp.where(inside, dot(after, inside.astype(F32).astype(BF16)), -1.0)
    attended = packet_ref[0, 0:slots, :].astype(F32)
    gates = mine_ref[:, 0:width].astype(F32)
    residual = mine_ref[:, width:].astype(F32)
    spots = lax.broadcasted_iota(jnp.int32, (slots, held), 1).astype(F32)
    for m in range(1, ctx_size):
        got = others[m - 1]
        attended = attended + got[0:slots, :].astype(F32)
        pick = (spots == rank[:, m : m + 1]).astype(F32).astype(BF16)
        gates = gates + dot(pick, got[slots : slots + held, :])
        residual = residual + dot(pick, got[slots + held :, :])
    residual_ref[...] = residual.astype(BF16)
    parts = []
    for at in range(0, width, HEAD_DIM):
        one = attended[:, at : at + HEAD_DIM]
        center = one - jnp.mean(one, axis=1, keepdims=True)
        parts.append(
            center
            * lax.rsqrt(jnp.mean(center * center, axis=1, keepdims=True) + 1e-05)
            * gates[:, at : at + HEAD_DIM]
        )
    hidden = jnp.concatenate(parts, axis=1).astype(BF16)
    for t in range(head_size):
        first = pl.multiple_of((me_head ^ t) * width, width)
        outs[t][...] = dot(hidden, weight_ref[:, pl.ds(first, width)]).astype(outs[t].dtype)


def final_kernel(head_size, *refs):
    count_ref = refs[0]
    parts = refs[1 : 1 + head_size]
    residual_ref, out_ref = refs[1 + head_size :]
    slots = residual_ref.shape[0]
    total = residual_ref[...].astype(F32)
    for part in parts:
        total = total + part[...].astype(F32)
    slot = lax.axis_index("ctx") * slots + lax.broadcasted_iota(jnp.int32, total.shape, 0)
    out_ref[...] = jnp.where(slot < count_ref[0], total, 0.0).astype(BF16)


def swap(x, axis, k):
    return lax.ppermute(x, axis, [(i, i ^ k) for i in range(lax.axis_size(axis))])


def on_device(
    counts, cand_owner, cand_row, item_table, proj_weight, out_weight, key_cache, value_cache
):
    users = lax.axis_size("users")
    ctx_size = lax.axis_size("ctx")
    head_size = lax.axis_size("head")
    slots = cand_row.shape[1]
    rows, model = item_table.shape
    width = proj_weight.shape[2]
    span = rows + PAD
    history = key_cache.shape[1] * ctx_size
    capacity = max(2, 2 * slots // (users * ctx_size))
    held = max(PAD, -(-users * min(capacity, slots) // PAD) * PAD)
    owner = cand_owner.reshape(1, slots)
    packet, normed = call(
        queries_kernel, (shape((span, width)), shape((rows, model))), name="queries"
    )(owner, cand_row, item_table, proj_weight[:, 2, :])
    pair = [packet] + [swap(packet, "users", k) for k in range(1, users)]
    bulk = call(rest_kernel, shape((rows, 3 * width)), name="rest")(
        normed, proj_weight.reshape(model, 4 * width), packet, item_table
    )
    bulks = [bulk] + [swap(bulk, "users", k) for k in range(1, users)]
    group = jnp.concatenate(pair, axis=0)
    groups = [group] + [swap(group, "ctx", m) for m in range(1, ctx_size)]
    size = slots + 2 * held
    sums, mine = call(
        lambda *refs: attend_kernel(users, ctx_size, held, history, *refs),
        (shape((ctx_size, size, width)), shape((slots, 2 * width))),
        scratch=(
            pltpu.VMEM((ctx_size * slots, width), BF16),
            pltpu.VMEM((ctx_size, width, PAD), F32),
            pltpu.VMEM((ctx_size * slots, width), F32),
        ),
        name="attend",
    )(*groups, *bulks, key_cache[0], value_cache[0])
    others = [swap(sums[m], "ctx", m) for m in range(1, ctx_size)]
    *parts, residual = call(
        lambda *refs: mix_kernel(users, ctx_size, head_size, held, *refs),
        (shape((slots, width), F32),) + (shape((slots, width)),) * (head_size - 1) + (shape((slots, width)),),
        name="mix",
    )(owner, sums, mine, *others, out_weight)
    got = [parts[0]] + [swap(parts[t], "head", t) for t in range(1, head_size)]
    specs = [pl.BlockSpec(memory_space=pltpu.SMEM)] + [vmem()] * (head_size + 1)
    out = pl.pallas_call(
        lambda *refs: final_kernel(head_size, *refs),
        out_shape=shape((slots, width)),
        in_specs=specs,
        out_specs=vmem(),
        name="final",
    )(counts, *got, residual)
    return out[None]


def solution(mesh):
    return jax.shard_map(
        on_device,
        mesh=mesh,
        in_specs=(
            P("users"),
            P("users", "ctx", None),
            P("users", "ctx"),
            P(("users", "ctx"), None),
            P(None, None, "head"),
            P("head", None),
            P("users", "ctx", "head"),
            P("users", "ctx", "head"),
        ),
        out_specs=P("users", "ctx", "head"),
        check_vma=False,
    )
```

```python
import jax
import jax.numpy as jnp
from jax import lax
from jax.experimental import pallas as pl
from jax.experimental.pallas import tpu as pltpu
from jax.sharding import PartitionSpec as P


HEAD_DIM = 128
PAD = 16
F32 = jnp.float32
BF16 = jnp.bfloat16


def silu(v):
    return 0.5 * v * (1.0 + jnp.tanh(0.5 * v))


def dot(a, b):
    return jnp.dot(a, b, preferred_element_type=F32)


def vmem():
    return pl.BlockSpec(memory_space=pltpu.VMEM)


def call(kernel, outs, scratch=(), specs=None):
    given = {} if specs is None else {"in_specs": specs}
    return pl.pallas_call(
        kernel, out_shape=outs, out_specs=jax.tree.map(lambda _: vmem(), outs), scratch_shapes=list(scratch), **given
    )


def shape(dims, kind=BF16):
    return jax.ShapeDtypeStruct(dims, kind)


def normed_of(table_ref):
    x = table_ref[...].astype(F32)
    center = x - jnp.mean(x, axis=1, keepdims=True)
    return (center * lax.rsqrt(jnp.mean(center * center, axis=1, keepdims=True) + 1e-05)).astype(BF16)


def project_kernel(owner_ref, row_ref, table_ref, weight_hbm, packet_ref, bulk_ref, weight_ref, sems):
    rows, model = table_ref.shape
    kinds, width = weight_ref.shape[1:]
    slots = owner_ref.shape[1]
    step = model // sems.shape[0]
    lanes = 128 * kinds
    copies = [
        pltpu.make_async_copy(weight_hbm.at[at : at + step], weight_ref.at[at : at + step], sems.at[at // step])
        for at in range(0, model, step)
    ]
    for one in copies:
        one.start()
    packet_ref[rows:, 0:slots] = jnp.broadcast_to(owner_ref[...].astype(F32), (PAD, slots)).astype(BF16)
    packet_ref[rows:, slots : 2 * slots] = jnp.broadcast_to(row_ref[...].astype(F32), (PAD, slots)).astype(BF16)
    start = pl.multiple_of(lax.axis_index("head") * width, width)
    bulk_ref[2 * rows : 3 * rows, :] = table_ref[:, pl.ds(start, width)]
    normed = normed_of(table_ref)
    spread = (
        lax.broadcasted_iota(jnp.int32, (128, lanes), 1) // kinds
        == lax.broadcasted_iota(jnp.int32, (128, lanes), 0)
    ).astype(F32).astype(BF16)
    kind = lax.broadcasted_iota(jnp.int32, (rows, lanes), 1) % kinds
    masks = [(kind == k).astype(F32).astype(BF16) for k in range(kinds)]
    total = jnp.zeros((kinds * rows, width), F32)
    for at in range(0, model, 128):
        wide = dot(normed[:, at : at + 128], spread).astype(BF16)
        left = jnp.concatenate([wide * mask for mask in masks], axis=0)
        if at % step == 0:
            copies[at // step].wait()
        total = total + dot(left, weight_ref[at : at + 128].reshape(lanes, width))
    gates, values, queries, keys = [silu(total[k * rows : (k + 1) * rows]).astype(BF16) for k in range(kinds)]
    packet_ref[0:rows, :] = queries
    bulk_ref[rows : 2 * rows, :] = gates
    bulk_ref[3 * rows :, :] = queries
    product = queries.astype(F32) * keys.astype(F32)
    for first in range(0, width, HEAD_DIM):
        cols = slice(first, first + HEAD_DIM)
        score = jnp.sum(product[:, cols], axis=1, keepdims=True)
        bulk_ref[0:rows, cols] = (silu(score * HEAD_DIM ** (-0.5)) * values[:, cols].astype(F32)).astype(BF16)


def one_hot(spot, size):
    lanes = lax.broadcasted_iota(jnp.int32, (spot.shape[0], size), 1).astype(F32)
    return (lanes == spot).astype(F32).astype(BF16)


def loop(size, body):
    if size <= 4:
        for j in range(size):
            body(j)
    else:
        lax.fori_loop(0, size, lambda j, c: (body(j), c)[1], 0)


def sort_kernel(users, ctx_size, held, *refs):
    packets = refs[:ctx_size]
    bulks = refs[ctx_size : ctx_size + users]
    outs = refs[ctx_size + users :]
    sends = outs[: ctx_size - 1]
    mine_ref, own_ref, query_ref, spot_ref, id_ref = outs[ctx_size - 1 :]
    me_user = lax.axis_index("users")
    me_ctx = lax.axis_index("ctx")
    rows = bulks[0].shape[0] // 4
    width = bulks[0].shape[1]
    slots = mine_ref.shape[0]
    owners = [
        [((me_user ^ k) * ctx_size + (me_ctx ^ m)).astype(F32) for m in range(ctx_size)] for k in range(users)
    ]
    for m in range(ctx_size):
        id_ref[m] = jnp.transpose(packets[m][rows:, :].astype(F32))
    lane = lax.broadcasted_iota(jnp.int32, (slots, 128), 1)

    def place(j):
        owner = id_ref[j, 0:slots, 0:1]
        row = id_ref[j, slots : 2 * slots, 0:1]
        spots = jnp.full((slots, 128), -1.0, F32)
        group = jnp.full((slots, 1), -1.0, F32)
        for k in range(users):
            spot = jnp.full((slots, 1), -1.0, F32)
            for m in range(ctx_size):
                spot = jnp.where(owner == owners[k][m], row + float(m * rows), spot)
            spots = jnp.where(lane == k, spot, spots)
            group = jnp.where(owner == owners[k][0], row + float(k * rows), group)
        first = j * slots if isinstance(j, int) else pl.multiple_of(j * slots, slots)
        spot_ref[pl.ds(first, slots), :] = spots
        pick = one_hot(spots[:, 0:1], ctx_size * rows)
        total = jnp.zeros((slots, width), F32)
        for m in range(ctx_size):
            total = total + dot(pick[:, m * rows : (m + 1) * rows], packets[m][0:rows, :])
        query_ref[pl.ds(first, slots), :] = total.astype(BF16)
        pick = one_hot(group, users * rows)
        own = jnp.zeros((slots, width), F32)
        for k in range(users):
            own = own + dot(pick[:, k * rows : (k + 1) * rows], bulks[k][0:rows, :])
        own_ref[pl.ds(first, slots), :] = own.astype(BF16)

    loop(ctx_size, place)
    before = (
        lax.broadcasted_iota(jnp.int32, (slots, slots), 0) < lax.broadcasted_iota(jnp.int32, (slots, slots), 1)
    ).astype(F32).astype(BF16)
    for j in range(ctx_size):
        owner = id_ref[j, 0:slots, 0:1]
        row = id_ref[j, slots : 2 * slots, 0:1]
        group = jnp.full((slots, 1), -1.0, F32)
        for k in range(users):
            group = jnp.where(owner == owners[k][0], row + float(k * rows), group)
        pick = one_hot(group, users * rows)
        if j > 0:
            line = packets[j][rows:, 0:slots].astype(F32)
            inside = jnp.zeros(line.shape, jnp.bool_)
            for k in range(users):
                inside = inside | (line == owners[k][0])
            rank = jnp.where(inside, dot(inside.astype(F32).astype(BF16), before), -1.0)[0:1, :]
            keep = lax.broadcasted_iota(jnp.int32, (held, slots), 0).astype(F32) == rank
            pick = dot(keep.astype(F32).astype(BF16), pick).astype(BF16)
        for part in range(2):
            total = jnp.zeros((pick.shape[0], width), F32)
            for k in range(users):
                total = total + dot(
                    pick[:, k * rows : (k + 1) * rows], bulks[k][(part + 1) * rows : (part + 2) * rows, :]
                )
            if j > 0:
                sends[j - 1][part * held : (part + 1) * held, :] = total.astype(BF16)
            else:
                mine_ref[:, part * width : (part + 1) * width] = total.astype(BF16)


def attend_kernel(users, ctx_size, rows, history, places, *refs):
    spot_ref, part_ref, own_ref, key_ref, value_ref = refs[:5]
    packs = refs[5 : 4 + ctx_size]
    outs = refs[-ctx_size - 2 : -2]
    others = refs[4 + ctx_size : -ctx_size - 2]
    query_ref, sum_ref = refs[-2:]
    width = key_ref.shape[1]
    slots = outs[0].shape[0]

    def place(j):
        first = j * slots if isinstance(j, int) else pl.multiple_of(j * slots, slots)
        total = part_ref[pl.ds(first, slots), :].astype(F32)
        for k in range(1, users):
            pick = one_hot(spot_ref[pl.ds(first, slots), k : k + 1], ctx_size * rows)
            for m in range(ctx_size):
                which, at = places[k, m]
                total = total + dot(pick[:, m * rows : (m + 1) * rows], others[which][at : at + rows, :])
        query_ref[pl.ds(first, slots), :] = total.astype(BF16)

    loop(ctx_size, place)
    count = ctx_size * slots
    block = min(count, 512)

    def attend(b):
        first = b * block if isinstance(b, int) else pl.multiple_of(b * block, block)
        for at in range(0, width, HEAD_DIM):
            cols = slice(at, at + HEAD_DIM)
            scores = lax.dot_general(
                query_ref[pl.ds(first, block), cols], key_ref[:, cols],
                (((1,), (1,)), ((), ())), preferred_element_type=F32,
            ) * (0.5 * HEAD_DIM ** (-0.5))
            weights = (scores + scores * jnp.tanh(scores)).astype(BF16)
            sum_ref[pl.ds(first, block), cols] = dot(weights, value_ref[:, cols])

    loop(count // block, attend)
    for j in range(ctx_size):
        span = slice(j * slots, (j + 1) * slots)
        outs[j][0:slots, :] = (sum_ref[span, :] * history ** (-0.5) + own_ref[span, :].astype(F32)).astype(BF16)
        if j > 0:
            outs[j][slots:, :] = packs[j - 1][...]


def mix_kernel(users, ctx_size, head_size, held, *refs):
    owner_ref, mine_ref, weight_ref = refs[:3]
    sums = refs[3 : 3 + ctx_size]
    outs = refs[3 + ctx_size : 3 + ctx_size + head_size]
    residual_ref = refs[3 + ctx_size + head_size]
    me_user = lax.axis_index("users")
    me_ctx = lax.axis_index("ctx")
    me_head = lax.axis_index("head")
    slots, width = mine_ref.shape[0], mine_ref.shape[1] // 2
    owner = jnp.transpose(jnp.broadcast_to(owner_ref[...].astype(F32), (8, slots)))[:, 0:1]
    lanes = 128
    lane = lax.broadcasted_iota(jnp.int32, (slots, lanes), 1)
    inside = jnp.zeros((slots, lanes), jnp.bool_)
    for k in range(users):
        named = (me_user ^ k) * ctx_size + (me_ctx ^ lane)
        inside = inside | ((owner == named.astype(F32)) & (lane < ctx_size))
    after = (
        lax.broadcasted_iota(jnp.int32, (slots, slots), 1) < lax.broadcasted_iota(jnp.int32, (slots, slots), 0)
    ).astype(F32).astype(BF16)
    rank = jnp.where(inside, dot(after, inside.astype(F32).astype(BF16)), -1.0)
    attended = sums[0][...].astype(F32)
    gates = mine_ref[:, 0:width].astype(F32)
    residual = mine_ref[:, width:].astype(F32)
    spots = lax.broadcasted_iota(jnp.int32, (slots, held), 1).astype(F32)
    for m in range(1, ctx_size):
        attended = attended + sums[m][0:slots, :].astype(F32)
        pick = (spots == rank[:, m : m + 1]).astype(F32).astype(BF16)
        gates = gates + dot(pick, sums[m][slots : slots + held, :])
        residual = residual + dot(pick, sums[m][slots + held :, :])
    residual_ref[...] = residual.astype(BF16)
    parts = []
    for at in range(0, width, HEAD_DIM):
        one = attended[:, at : at + HEAD_DIM]
        center = one - jnp.mean(one, axis=1, keepdims=True)
        parts.append(
            center
            * lax.rsqrt(jnp.mean(center * center, axis=1, keepdims=True) + 1e-05)
            * gates[:, at : at + HEAD_DIM]
        )
    hidden = jnp.concatenate(parts, axis=1).astype(BF16)
    for t in range(head_size):
        first = pl.multiple_of((me_head ^ t) * width, width)
        outs[t][...] = dot(hidden, weight_ref[:, pl.ds(first, width)]).astype(outs[t].dtype)


def swap(x, axis, k):
    return lax.ppermute(x, axis, [(i, i ^ k) for i in range(lax.axis_size(axis))])


def layer(
    counts, cand_owner, cand_row, item_table, proj_weight, out_weight, key_cache, value_cache
):
    users = lax.axis_size("users")
    ctx_size = lax.axis_size("ctx")
    head_size = lax.axis_size("head")
    slots = cand_row.shape[1]
    rows, model = item_table.shape
    width = proj_weight.shape[2]
    span = rows + PAD
    history = key_cache.shape[1] * ctx_size
    capacity = max(2, 2 * slots // (users * ctx_size))
    held = max(PAD, -(-users * min(capacity, slots) // PAD) * PAD)
    owner = cand_owner.reshape(1, slots)
    kinds = proj_weight.shape[1]
    stage = (pltpu.VMEM((model, kinds, width), BF16), pltpu.SemaphoreType.DMA((4,)))
    hbm = pl.BlockSpec(memory_space=pl.ANY)
    packet, bulk = call(
        project_kernel, (shape((span, width)), shape((4 * rows, width))), stage, specs=[vmem()] * 3 + [hbm]
    )(owner, cand_row, item_table, proj_weight)
    packets = [packet] + [swap(packet, "ctx", m) for m in range(1, ctx_size)]
    bulks = [bulk] + [swap(bulk, "users", k) for k in range(1, users)]
    relays, places = [], {}
    for k in range(1, users):
        places[k, 0] = (len(relays), 3 * rows)
        relays.append(bulks[k])
    if users * ctx_size <= 8:
        for m in range(1, ctx_size):
            for k in range(1, users):
                places[k, m] = (len(relays), 0)
                relays.append(swap(packets[m], "users", k))
    elif ctx_size > 1:
        joined = jnp.concatenate(packets[1:], axis=0)
        for k in range(1, users):
            for m in range(1, ctx_size):
                places[k, m] = (len(relays), (m - 1) * span)
            relays.append(swap(joined, "users", k))
    count = ctx_size * slots
    *packs, mine, own, part, spots = call(
        lambda *refs: sort_kernel(users, ctx_size, held, *refs),
        (shape((2 * held, width)),) * (ctx_size - 1)
        + (shape((slots, 2 * width)), shape((count, width)), shape((count, width)), shape((count, 128), F32)),
        (pltpu.VMEM((ctx_size, width, PAD), F32),),
    )(*packets, *bulks)
    sums = call(
        lambda *refs: attend_kernel(users, ctx_size, rows, history, places, *refs),
        (shape((slots, width)),) + (shape((slots + 2 * held, width)),) * (ctx_size - 1),
        (pltpu.VMEM((count, width), BF16), pltpu.VMEM((count, width), F32)),
    )(spots, part, own, key_cache[0], value_cache[0], *packs, *relays)
    sums = [sums[0]] + [swap(sums[m], "ctx", m) for m in range(1, ctx_size)]
    *parts, residual = call(
        lambda *refs: mix_kernel(users, ctx_size, head_size, held, *refs),
        (shape((slots, width), F32),) + (shape((slots, width)),) * (head_size - 1) + (shape((slots, width)),),
    )(owner, mine, out_weight, *sums)
    got = [parts[0]] + [swap(parts[t], "head", t) for t in range(1, head_size)]
    total = residual.astype(F32)
    for one in got:
        total = total + one.astype(F32)
    slot = lax.axis_index("ctx") * slots + jnp.arange(slots, dtype=jnp.int32)
    return jnp.where((slot < counts[0])[:, None], total, 0.0).astype(BF16)[None]


def solution(mesh):
    return jax.shard_map(
        layer,
        mesh=mesh,
        in_specs=(
            P("users"),
            P("users", "ctx", None),
            P("users", "ctx"),
            P(("users", "ctx"), None),
            P(None, None, "head"),
            P("head", None),
            P("users", "ctx", "head"),
            P("users", "ctx", "head"),
        ),
        out_specs=P("users", "ctx", "head"),
        check_vma=False,
    )
```

```python
import jax
import jax.numpy as jnp
from jax import lax
from jax.experimental import pallas as pl
from jax.experimental.pallas import tpu as pltpu
from jax.sharding import PartitionSpec as P


HEAD_DIM = 128
PAD = 16
F32 = jnp.float32
BF16 = jnp.bfloat16


def silu(v):
    return 0.5 * v * (1.0 + jnp.tanh(0.5 * v))


def dot(a, b):
    return jnp.dot(a, b, preferred_element_type=F32)


def vmem():
    return pl.BlockSpec(memory_space=pltpu.VMEM)


def call(kernel, outs, scratch=(), specs=None, far=()):
    given = {} if specs is None else {"in_specs": specs}
    made = pl.pallas_call(
        kernel,
        out_shape=jax.tree.map(lambda o: pltpu.VMEM(o.shape, o.dtype), outs),
        out_specs=jax.tree.map(lambda _: vmem(), outs),
        scratch_shapes=list(scratch),
        compiler_params=pltpu.CompilerParams(vmem_limit_bytes=16 << 20),
        **given,
    )

    def run(*args):
        spaces = [pltpu.HBM if i in far else pltpu.VMEM for i in range(len(args))]
        args = [pltpu.with_memory_space_constraint(x, space) for x, space in zip(args, spaces)]
        return made(*args)

    return run


def shape(dims, kind=BF16):
    return jax.ShapeDtypeStruct(dims, kind)


def normed_of(table_ref):
    x = table_ref[...].astype(F32)
    center = x - jnp.mean(x, axis=1, keepdims=True)
    return (center * lax.rsqrt(jnp.mean(center * center, axis=1, keepdims=True) + 1e-05)).astype(BF16)


def project_kernel(owner_ref, row_ref, table_ref, weight_hbm, packet_ref, bulk_ref, weight_ref, sems):
    rows, model = table_ref.shape
    kinds, width = weight_ref.shape[1:]
    slots = owner_ref.shape[1]
    step = model // sems.shape[0]
    lanes = 128 * kinds
    copies = [
        pltpu.make_async_copy(weight_hbm.at[at : at + step], weight_ref.at[at : at + step], sems.at[at // step])
        for at in range(0, model, step)
    ]
    for one in copies:
        one.start()
    packet_ref[rows:, 0:slots] = jnp.broadcast_to(owner_ref[...].astype(F32), (PAD, slots)).astype(BF16)
    packet_ref[rows:, slots : 2 * slots] = jnp.broadcast_to(row_ref[...].astype(F32), (PAD, slots)).astype(BF16)
    start = pl.multiple_of(lax.axis_index("head") * width, width)
    bulk_ref[2 * rows : 3 * rows, :] = table_ref[:, pl.ds(start, width)]
    normed = normed_of(table_ref)
    spread = (
        lax.broadcasted_iota(jnp.int32, (128, lanes), 1) // kinds
        == lax.broadcasted_iota(jnp.int32, (128, lanes), 0)
    ).astype(F32).astype(BF16)
    kind = lax.broadcasted_iota(jnp.int32, (rows, lanes), 1) % kinds
    masks = [(kind == k).astype(F32).astype(BF16) for k in range(kinds)]
    total = jnp.zeros((kinds * rows, width), F32)
    for at in range(0, model, 128):
        wide = dot(normed[:, at : at + 128], spread).astype(BF16)
        left = jnp.concatenate([wide * mask for mask in masks], axis=0)
        if at % step == 0:
            copies[at // step].wait()
        total = total + dot(left, weight_ref[at : at + 128].reshape(lanes, width))
    gates, values, queries, keys = [silu(total[k * rows : (k + 1) * rows]).astype(BF16) for k in range(kinds)]
    packet_ref[0:rows, :] = queries
    bulk_ref[rows : 2 * rows, :] = gates
    bulk_ref[3 * rows :, :] = queries
    product = queries.astype(F32) * keys.astype(F32)
    for first in range(0, width, HEAD_DIM):
        cols = slice(first, first + HEAD_DIM)
        score = jnp.sum(product[:, cols], axis=1, keepdims=True)
        bulk_ref[0:rows, cols] = (silu(score * HEAD_DIM ** (-0.5)) * values[:, cols].astype(F32)).astype(BF16)


def one_hot(spot, size):
    lanes = lax.broadcasted_iota(jnp.int32, (spot.shape[0], size), 1).astype(F32)
    return (lanes == spot).astype(F32).astype(BF16)


def loop(size, body):
    if size <= 4:
        for j in range(size):
            body(j)
    else:
        lax.fori_loop(0, size, lambda j, c: (body(j), c)[1], 0)


def sort_kernel(users, ctx_size, held, *refs):
    packets = refs[:ctx_size]
    bulks = refs[ctx_size : ctx_size + users]
    outs = refs[ctx_size + users :]
    sends = outs[: ctx_size - 1]
    mine_ref, own_ref, query_ref, spot_ref, id_ref = outs[ctx_size - 1 :]
    me_user = lax.axis_index("users")
    me_ctx = lax.axis_index("ctx")
    rows = bulks[0].shape[0] // 4
    width = bulks[0].shape[1]
    slots = mine_ref.shape[0]
    owners = [
        [((me_user ^ k) * ctx_size + (me_ctx ^ m)).astype(F32) for m in range(ctx_size)] for k in range(users)
    ]
    for m in range(ctx_size):
        id_ref[m] = jnp.transpose(packets[m][rows:, :].astype(F32))
    lane = lax.broadcasted_iota(jnp.int32, (slots, 128), 1)

    def place(j):
        owner = id_ref[j, 0:slots, 0:1]
        row = id_ref[j, slots : 2 * slots, 0:1]
        spots = jnp.full((slots, 128), -1.0, F32)
        group = jnp.full((slots, 1), -1.0, F32)
        for k in range(users):
            spot = jnp.full((slots, 1), -1.0, F32)
            for m in range(ctx_size):
                spot = jnp.where(owner == owners[k][m], row + float(m * rows), spot)
            spots = jnp.where(lane == k, spot, spots)
            group = jnp.where(owner == owners[k][0], row + float(k * rows), group)
        first = j * slots if isinstance(j, int) else pl.multiple_of(j * slots, slots)
        spot_ref[pl.ds(first, slots), :] = spots
        pick = one_hot(spots[:, 0:1], ctx_size * rows)
        total = jnp.zeros((slots, width), F32)
        for m in range(ctx_size):
            total = total + dot(pick[:, m * rows : (m + 1) * rows], packets[m][0:rows, :])
        query_ref[pl.ds(first, slots), :] = total.astype(BF16)
        pick = one_hot(group, users * rows)
        own = jnp.zeros((slots, width), F32)
        for k in range(users):
            own = own + dot(pick[:, k * rows : (k + 1) * rows], bulks[k][0:rows, :])
        own_ref[pl.ds(first, slots), :] = own.astype(BF16)

    loop(ctx_size, place)
    before = (
        lax.broadcasted_iota(jnp.int32, (slots, slots), 0) < lax.broadcasted_iota(jnp.int32, (slots, slots), 1)
    ).astype(F32).astype(BF16)
    for j in range(ctx_size):
        owner = id_ref[j, 0:slots, 0:1]
        row = id_ref[j, slots : 2 * slots, 0:1]
        group = jnp.full((slots, 1), -1.0, F32)
        for k in range(users):
            group = jnp.where(owner == owners[k][0], row + float(k * rows), group)
        pick = one_hot(group, users * rows)
        if j > 0:
            line = packets[j][rows:, 0:slots].astype(F32)
            inside = jnp.zeros(line.shape, jnp.bool_)
            for k in range(users):
                inside = inside | (line == owners[k][0])
            rank = jnp.where(inside, dot(inside.astype(F32).astype(BF16), before), -1.0)[0:1, :]
            keep = lax.broadcasted_iota(jnp.int32, (held, slots), 0).astype(F32) == rank
            pick = dot(keep.astype(F32).astype(BF16), pick).astype(BF16)
        for part in range(2):
            total = jnp.zeros((pick.shape[0], width), F32)
            for k in range(users):
                total = total + dot(
                    pick[:, k * rows : (k + 1) * rows], bulks[k][(part + 1) * rows : (part + 2) * rows, :]
                )
            if j > 0:
                sends[j - 1][part * held : (part + 1) * held, :] = total.astype(BF16)
            else:
                mine_ref[:, part * width : (part + 1) * width] = total.astype(BF16)


def attend_kernel(users, ctx_size, rows, history, places, *refs):
    spot_ref, part_ref, own_ref, key_ref, value_ref = refs[:5]
    packs = refs[5 : 4 + ctx_size]
    outs = refs[-ctx_size - 2 : -2]
    others = refs[4 + ctx_size : -ctx_size - 2]
    query_ref, sum_ref = refs[-2:]
    width = key_ref.shape[1]
    slots = outs[0].shape[0]

    def place(j):
        first = j * slots if isinstance(j, int) else pl.multiple_of(j * slots, slots)
        total = part_ref[pl.ds(first, slots), :].astype(F32)
        for k in range(1, users):
            pick = one_hot(spot_ref[pl.ds(first, slots), k : k + 1], ctx_size * rows)
            for m in range(ctx_size):
                which, at = places[k, m]
                total = total + dot(pick[:, m * rows : (m + 1) * rows], others[which][at : at + rows, :])
        query_ref[pl.ds(first, slots), :] = total.astype(BF16)

    loop(ctx_size, place)
    count = ctx_size * slots
    block = min(count, 512)

    def attend(b):
        first = b * block if isinstance(b, int) else pl.multiple_of(b * block, block)
        for at in range(0, width, HEAD_DIM):
            cols = slice(at, at + HEAD_DIM)
            scores = lax.dot_general(
                query_ref[pl.ds(first, block), cols], key_ref[:, cols],
                (((1,), (1,)), ((), ())), preferred_element_type=F32,
            ) * (0.5 * HEAD_DIM ** (-0.5))
            weights = (scores + scores * jnp.tanh(scores)).astype(BF16)
            sum_ref[pl.ds(first, block), cols] = dot(weights, value_ref[:, cols])

    loop(count // block, attend)
    for j in range(ctx_size):
        span = slice(j * slots, (j + 1) * slots)
        outs[j][0:slots, :] = (sum_ref[span, :] * history ** (-0.5) + own_ref[span, :].astype(F32)).astype(BF16)
        if j > 0:
            outs[j][slots:, :] = packs[j - 1][...]


def mix_kernel(users, ctx_size, head_size, held, *refs):
    owner_ref, mine_ref, weight_ref = refs[:3]
    sums = refs[3 : 3 + ctx_size]
    outs = refs[3 + ctx_size : 3 + ctx_size + head_size]
    residual_ref = refs[3 + ctx_size + head_size]
    me_user = lax.axis_index("users")
    me_ctx = lax.axis_index("ctx")
    me_head = lax.axis_index("head")
    slots, width = mine_ref.shape[0], mine_ref.shape[1] // 2
    owner = jnp.transpose(jnp.broadcast_to(owner_ref[...].astype(F32), (8, slots)))[:, 0:1]
    lanes = 128
    lane = lax.broadcasted_iota(jnp.int32, (slots, lanes), 1)
    inside = jnp.zeros((slots, lanes), jnp.bool_)
    for k in range(users):
        named = (me_user ^ k) * ctx_size + (me_ctx ^ lane)
        inside = inside | ((owner == named.astype(F32)) & (lane < ctx_size))
    after = (
        lax.broadcasted_iota(jnp.int32, (slots, slots), 1) < lax.broadcasted_iota(jnp.int32, (slots, slots), 0)
    ).astype(F32).astype(BF16)
    rank = jnp.where(inside, dot(after, inside.astype(F32).astype(BF16)), -1.0)
    attended = sums[0][...].astype(F32)
    gates = mine_ref[:, 0:width].astype(F32)
    residual = mine_ref[:, width:].astype(F32)
    spots = lax.broadcasted_iota(jnp.int32, (slots, held), 1).astype(F32)
    for m in range(1, ctx_size):
        attended = attended + sums[m][0:slots, :].astype(F32)
        pick = (spots == rank[:, m : m + 1]).astype(F32).astype(BF16)
        gates = gates + dot(pick, sums[m][slots : slots + held, :])
        residual = residual + dot(pick, sums[m][slots + held :, :])
    residual_ref[...] = residual.astype(BF16)
    parts = []
    for at in range(0, width, HEAD_DIM):
        one = attended[:, at : at + HEAD_DIM]
        center = one - jnp.mean(one, axis=1, keepdims=True)
        parts.append(
            center
            * lax.rsqrt(jnp.mean(center * center, axis=1, keepdims=True) + 1e-05)
            * gates[:, at : at + HEAD_DIM]
        )
    hidden = jnp.concatenate(parts, axis=1).astype(BF16)
    for t in range(head_size):
        first = pl.multiple_of((me_head ^ t) * width, width)
        outs[t][...] = dot(hidden, weight_ref[:, pl.ds(first, width)]).astype(outs[t].dtype)


def swap(x, axis, k):
    return lax.ppermute(x, axis, [(i, i ^ k) for i in range(lax.axis_size(axis))])


def layer(
    counts, cand_owner, cand_row, item_table, proj_weight, out_weight, key_cache, value_cache
):
    users = lax.axis_size("users")
    ctx_size = lax.axis_size("ctx")
    head_size = lax.axis_size("head")
    slots = cand_row.shape[1]
    rows, model = item_table.shape
    width = proj_weight.shape[2]
    span = rows + PAD
    history = key_cache.shape[1] * ctx_size
    capacity = max(2, 2 * slots // (users * ctx_size))
    held = max(PAD, -(-users * min(capacity, slots) // PAD) * PAD)
    owner = cand_owner.reshape(1, slots)
    kinds = proj_weight.shape[1]
    stage = (pltpu.VMEM((model, kinds, width), BF16), pltpu.SemaphoreType.DMA((4,)))
    hbm = pl.BlockSpec(memory_space=pl.ANY)
    packet, bulk = call(
        project_kernel,
        (shape((span, width)), shape((4 * rows, width))),
        stage,
        specs=[vmem()] * 3 + [hbm],
        far=(0, 1, 2, 3),
    )(owner, cand_row, item_table, proj_weight)
    packets = [packet] + [swap(packet, "ctx", m) for m in range(1, ctx_size)]
    bulks = [bulk] + [swap(bulk, "users", k) for k in range(1, users)]
    relays, places = [], {}
    for k in range(1, users):
        places[k, 0] = (len(relays), 3 * rows)
        relays.append(bulks[k])
    if users * ctx_size <= 8:
        for m in range(1, ctx_size):
            for k in range(1, users):
                places[k, m] = (len(relays), 0)
                relays.append(swap(packets[m], "users", k))
    elif ctx_size > 1:
        joined = jnp.concatenate(packets[1:], axis=0)
        for k in range(1, users):
            for m in range(1, ctx_size):
                places[k, m] = (len(relays), (m - 1) * span)
            relays.append(swap(joined, "users", k))
    count = ctx_size * slots
    *packs, mine, own, part, spots = call(
        lambda *refs: sort_kernel(users, ctx_size, held, *refs),
        (shape((2 * held, width)),) * (ctx_size - 1)
        + (shape((slots, 2 * width)), shape((count, width)), shape((count, width)), shape((count, 128), F32)),
        (pltpu.VMEM((ctx_size, width, PAD), F32),),
    )(*packets, *bulks)
    sums = call(
        lambda *refs: attend_kernel(users, ctx_size, rows, history, places, *refs),
        (shape((slots, width)),) + (shape((slots + 2 * held, width)),) * (ctx_size - 1),
        (pltpu.VMEM((count, width), BF16), pltpu.VMEM((count, width), F32)),
    )(spots, part, own, key_cache[0], value_cache[0], *packs, *relays)
    sums = [sums[0]] + [swap(sums[m], "ctx", m) for m in range(1, ctx_size)]
    *parts, residual = call(
        lambda *refs: mix_kernel(users, ctx_size, head_size, held, *refs),
        (shape((slots, width), F32),) + (shape((slots, width)),) * (head_size - 1) + (shape((slots, width)),),
    )(owner, mine, out_weight, *sums)
    got = [parts[0]] + [swap(parts[t], "head", t) for t in range(1, head_size)]
    total = residual.astype(F32)
    for one in got:
        total = total + one.astype(F32)
    slot = lax.broadcasted_iota(jnp.int32, total.shape, 0)
    return jnp.where(slot < counts[0] - lax.axis_index("ctx") * slots, total, 0.0).astype(BF16)[None]


def solution(mesh):
    return jax.shard_map(
        layer,
        mesh=mesh,
        in_specs=(
            P("users"),
            P("users", "ctx", None),
            P("users", "ctx"),
            P(("users", "ctx"), None),
            P(None, None, "head"),
            P("head", None),
            P("users", "ctx", "head"),
            P("users", "ctx", "head"),
        ),
        out_specs=P("users", "ctx", "head"),
        check_vma=False,
    )
```

```python
import jax
import jax.numpy as jnp
from jax import lax
from jax.experimental import pallas as pl
from jax.experimental.pallas import tpu as pltpu
from jax.sharding import PartitionSpec as P


HEAD_DIM = 128
PAD = 16
F32 = jnp.float32
BF16 = jnp.bfloat16


def silu(v):
    return 0.5 * v * (1.0 + jnp.tanh(0.5 * v))


def dot(a, b):
    return jnp.dot(a, b, preferred_element_type=F32)


def vmem():
    return pl.BlockSpec(memory_space=pltpu.VMEM)


def call(kernel, outs, scratch=(), specs=None, far=()):
    given = {} if specs is None else {"in_specs": specs}
    made = pl.pallas_call(
        kernel,
        out_shape=jax.tree.map(lambda o: pltpu.VMEM(o.shape, o.dtype), outs),
        out_specs=jax.tree.map(lambda _: vmem(), outs),
        scratch_shapes=list(scratch),
        compiler_params=pltpu.CompilerParams(vmem_limit_bytes=16 << 20),
        **given,
    )

    def run(*args):
        spaces = [pltpu.HBM if i in far else pltpu.VMEM for i in range(len(args))]
        args = [pltpu.with_memory_space_constraint(x, space) for x, space in zip(args, spaces)]
        return made(*args)

    return run


def shape(dims, kind=BF16):
    return jax.ShapeDtypeStruct(dims, kind)


def normed_of(table_ref):
    x = table_ref[...].astype(F32)
    center = x - jnp.mean(x, axis=1, keepdims=True)
    return (center * lax.rsqrt(jnp.mean(center * center, axis=1, keepdims=True) + 1e-05)).astype(BF16)


def project_kernel(owner_ref, row_ref, table_ref, weight_hbm, packet_ref, bulk_ref, weight_ref, sems):
    rows, model = table_ref.shape
    kinds, width = weight_ref.shape[1:]
    slots = owner_ref.shape[1]
    step = model // sems.shape[0]
    lanes = 128 * kinds
    copies = [
        pltpu.make_async_copy(weight_hbm.at[at : at + step], weight_ref.at[at : at + step], sems.at[at // step])
        for at in range(0, model, step)
    ]
    for one in copies:
        one.start()
    packet_ref[rows:, 0:slots] = jnp.broadcast_to(owner_ref[...].astype(F32), (PAD, slots)).astype(BF16)
    packet_ref[rows:, slots : 2 * slots] = jnp.broadcast_to(row_ref[...].astype(F32), (PAD, slots)).astype(BF16)
    start = pl.multiple_of(lax.axis_index("head") * width, width)
    bulk_ref[2 * rows : 3 * rows, :] = table_ref[:, pl.ds(start, width)]
    normed = normed_of(table_ref)
    spread = (
        lax.broadcasted_iota(jnp.int32, (128, lanes), 1) // kinds
        == lax.broadcasted_iota(jnp.int32, (128, lanes), 0)
    ).astype(F32).astype(BF16)
    kind = lax.broadcasted_iota(jnp.int32, (rows, lanes), 1) % kinds
    masks = [(kind == k).astype(F32).astype(BF16) for k in range(kinds)]
    total = jnp.zeros((kinds * rows, width), F32)
    for at in range(0, model, 128):
        wide = dot(normed[:, at : at + 128], spread).astype(BF16)
        left = jnp.concatenate([wide * mask for mask in masks], axis=0)
        if at % step == 0:
            copies[at // step].wait()
        total = total + dot(left, weight_ref[at : at + 128].reshape(lanes, width))
    gates, values, queries, keys = [silu(total[k * rows : (k + 1) * rows]).astype(BF16) for k in range(kinds)]
    packet_ref[0:rows, :] = queries
    bulk_ref[rows : 2 * rows, :] = gates
    bulk_ref[3 * rows :, :] = queries
    product = queries.astype(F32) * keys.astype(F32)
    for first in range(0, width, HEAD_DIM):
        cols = slice(first, first + HEAD_DIM)
        score = jnp.sum(product[:, cols], axis=1, keepdims=True)
        bulk_ref[0:rows, cols] = (silu(score * HEAD_DIM ** (-0.5)) * values[:, cols].astype(F32)).astype(BF16)


def one_hot(spot, size):
    lanes = lax.broadcasted_iota(jnp.int32, (spot.shape[0], size), 1).astype(F32)
    return (lanes == spot).astype(F32).astype(BF16)


def loop(size, body):
    if size <= 4:
        for j in range(size):
            body(j)
    else:
        lax.fori_loop(0, size, lambda j, c: (body(j), c)[1], 0)


def sort_kernel(users, ctx_size, held, *refs):
    packets = refs[:ctx_size]
    bulks = refs[ctx_size : ctx_size + users]
    outs = refs[ctx_size + users :]
    sends = outs[: ctx_size - 1]
    mine_ref, own_ref, query_ref, spot_ref, id_ref = outs[ctx_size - 1 :]
    me_user = lax.axis_index("users")
    me_ctx = lax.axis_index("ctx")
    rows = bulks[0].shape[0] // 4
    width = bulks[0].shape[1]
    slots = mine_ref.shape[0]
    owners = [
        [((me_user ^ k) * ctx_size + (me_ctx ^ m)).astype(F32) for m in range(ctx_size)] for k in range(users)
    ]
    for m in range(ctx_size):
        id_ref[m] = jnp.transpose(packets[m][rows:, :].astype(F32))
    lane = lax.broadcasted_iota(jnp.int32, (slots, 128), 1)

    def place(j):
        owner = id_ref[j, 0:slots, 0:1]
        row = id_ref[j, slots : 2 * slots, 0:1]
        spots = jnp.full((slots, 128), -1.0, F32)
        group = jnp.full((slots, 1), -1.0, F32)
        for k in range(users):
            spot = jnp.full((slots, 1), -1.0, F32)
            for m in range(ctx_size):
                spot = jnp.where(owner == owners[k][m], row + float(m * rows), spot)
            spots = jnp.where(lane == k, spot, spots)
            group = jnp.where(owner == owners[k][0], row + float(k * rows), group)
        first = j * slots if isinstance(j, int) else pl.multiple_of(j * slots, slots)
        spot_ref[pl.ds(first, slots), :] = spots
        pick = one_hot(spots[:, 0:1], ctx_size * rows)
        total = jnp.zeros((slots, width), F32)
        for m in range(ctx_size):
            total = total + dot(pick[:, m * rows : (m + 1) * rows], packets[m][0:rows, :])
        query_ref[pl.ds(first, slots), :] = total.astype(BF16)
        pick = one_hot(group, users * rows)
        own = jnp.zeros((slots, width), F32)
        for k in range(users):
            own = own + dot(pick[:, k * rows : (k + 1) * rows], bulks[k][0:rows, :])
        own_ref[pl.ds(first, slots), :] = own.astype(BF16)

    loop(ctx_size, place)
    before = (
        lax.broadcasted_iota(jnp.int32, (slots, slots), 0) < lax.broadcasted_iota(jnp.int32, (slots, slots), 1)
    ).astype(F32).astype(BF16)
    for j in range(ctx_size):
        owner = id_ref[j, 0:slots, 0:1]
        row = id_ref[j, slots : 2 * slots, 0:1]
        group = jnp.full((slots, 1), -1.0, F32)
        for k in range(users):
            group = jnp.where(owner == owners[k][0], row + float(k * rows), group)
        pick = one_hot(group, users * rows)
        if j > 0:
            line = packets[j][rows:, 0:slots].astype(F32)
            inside = jnp.zeros(line.shape, jnp.bool_)
            for k in range(users):
                inside = inside | (line == owners[k][0])
            rank = jnp.where(inside, dot(inside.astype(F32).astype(BF16), before), -1.0)[0:1, :]
            keep = lax.broadcasted_iota(jnp.int32, (held, slots), 0).astype(F32) == rank
            pick = dot(keep.astype(F32).astype(BF16), pick).astype(BF16)
        for part in range(2):
            total = jnp.zeros((pick.shape[0], width), F32)
            for k in range(users):
                total = total + dot(
                    pick[:, k * rows : (k + 1) * rows], bulks[k][(part + 1) * rows : (part + 2) * rows, :]
                )
            if j > 0:
                sends[j - 1][part * held : (part + 1) * held, :] = total.astype(BF16)
            else:
                mine_ref[:, part * width : (part + 1) * width] = total.astype(BF16)


def attend_kernel(users, ctx_size, rows, history, places, *refs):
    spot_ref, part_ref, own_ref, key_ref, value_ref = refs[:5]
    outs = refs[-ctx_size - 2 : -2]
    others = refs[5 : -ctx_size - 2]
    query_ref, sum_ref = refs[-2:]
    width = key_ref.shape[1]
    slots = outs[0].shape[0]

    def place(j):
        first = j * slots if isinstance(j, int) else pl.multiple_of(j * slots, slots)
        total = part_ref[pl.ds(first, slots), :].astype(F32)
        for k in range(1, users):
            pick = one_hot(spot_ref[pl.ds(first, slots), k : k + 1], ctx_size * rows)
            for m in range(ctx_size):
                which, at = places[k, m]
                total = total + dot(pick[:, m * rows : (m + 1) * rows], others[which][at : at + rows, :])
        query_ref[pl.ds(first, slots), :] = total.astype(BF16)

    loop(ctx_size, place)
    count = ctx_size * slots
    block = min(count, 512)

    def attend(b):
        first = b * block if isinstance(b, int) else pl.multiple_of(b * block, block)
        for at in range(0, width, HEAD_DIM):
            cols = slice(at, at + HEAD_DIM)
            scores = lax.dot_general(
                query_ref[pl.ds(first, block), cols], key_ref[:, cols],
                (((1,), (1,)), ((), ())), preferred_element_type=F32,
            ) * (0.5 * HEAD_DIM ** (-0.5))
            weights = (scores + scores * jnp.tanh(scores)).astype(BF16)
            sum_ref[pl.ds(first, block), cols] = dot(weights, value_ref[:, cols])

    loop(count // block, attend)
    for j in range(ctx_size):
        span = slice(j * slots, (j + 1) * slots)
        outs[j][...] = (sum_ref[span, :] * history ** (-0.5) + own_ref[span, :].astype(F32)).astype(BF16)


def mix_kernel(users, ctx_size, head_size, held, *refs):
    owner_ref, mine_ref, weight_ref = refs[:3]
    sums = refs[3 : 3 + ctx_size]
    packs = refs[3 + ctx_size : 2 + 2 * ctx_size]
    outs = refs[2 + 2 * ctx_size : 2 + 2 * ctx_size + head_size]
    residual_ref = refs[2 + 2 * ctx_size + head_size]
    me_user = lax.axis_index("users")
    me_ctx = lax.axis_index("ctx")
    me_head = lax.axis_index("head")
    slots, width = mine_ref.shape[0], mine_ref.shape[1] // 2
    owner = jnp.transpose(jnp.broadcast_to(owner_ref[...].astype(F32), (8, slots)))[:, 0:1]
    lanes = 128
    lane = lax.broadcasted_iota(jnp.int32, (slots, lanes), 1)
    inside = jnp.zeros((slots, lanes), jnp.bool_)
    for k in range(users):
        named = (me_user ^ k) * ctx_size + (me_ctx ^ lane)
        inside = inside | ((owner == named.astype(F32)) & (lane < ctx_size))
    after = (
        lax.broadcasted_iota(jnp.int32, (slots, slots), 1) < lax.broadcasted_iota(jnp.int32, (slots, slots), 0)
    ).astype(F32).astype(BF16)
    rank = jnp.where(inside, dot(after, inside.astype(F32).astype(BF16)), -1.0)
    attended = sums[0][...].astype(F32)
    gates = mine_ref[:, 0:width].astype(F32)
    residual = mine_ref[:, width:].astype(F32)
    spots = lax.broadcasted_iota(jnp.int32, (slots, held), 1).astype(F32)
    for m in range(1, ctx_size):
        attended = attended + sums[m][...].astype(F32)
        pick = (spots == rank[:, m : m + 1]).astype(F32).astype(BF16)
        gates = gates + dot(pick, packs[m - 1][0:held, :])
        residual = residual + dot(pick, packs[m - 1][held:, :])
    residual_ref[...] = residual.astype(BF16)
    parts = []
    for at in range(0, width, HEAD_DIM):
        one = attended[:, at : at + HEAD_DIM]
        center = one - jnp.mean(one, axis=1, keepdims=True)
        parts.append(
            center
            * lax.rsqrt(jnp.mean(center * center, axis=1, keepdims=True) + 1e-05)
            * gates[:, at : at + HEAD_DIM]
        )
    hidden = jnp.concatenate(parts, axis=1).astype(BF16)
    for t in range(head_size):
        first = pl.multiple_of((me_head ^ t) * width, width)
        outs[t][...] = dot(hidden, weight_ref[:, pl.ds(first, width)]).astype(outs[t].dtype)


def swap(x, axis, k):
    return lax.ppermute(x, axis, [(i, i ^ k) for i in range(lax.axis_size(axis))])


def layer(
    counts, cand_owner, cand_row, item_table, proj_weight, out_weight, key_cache, value_cache
):
    users = lax.axis_size("users")
    ctx_size = lax.axis_size("ctx")
    head_size = lax.axis_size("head")
    slots = cand_row.shape[1]
    rows, model = item_table.shape
    width = proj_weight.shape[2]
    span = rows + PAD
    history = key_cache.shape[1] * ctx_size
    capacity = max(2, 2 * slots // (users * ctx_size))
    held = max(PAD, -(-users * min(capacity, slots) // PAD) * PAD)
    owner = cand_owner.reshape(1, slots)
    kinds = proj_weight.shape[1]
    stage = (pltpu.VMEM((model, kinds, width), BF16), pltpu.SemaphoreType.DMA((4,)))
    hbm = pl.BlockSpec(memory_space=pl.ANY)
    packet, bulk = call(
        project_kernel,
        (shape((span, width)), shape((4 * rows, width))),
        stage,
        specs=[vmem()] * 3 + [hbm],
        far=(0, 1, 2, 3),
    )(owner, cand_row, item_table, proj_weight)
    packets = [packet] + [swap(packet, "ctx", m) for m in range(1, ctx_size)]
    bulks = [bulk] + [swap(bulk, "users", k) for k in range(1, users)]
    relays, places = [], {}
    for k in range(1, users):
        places[k, 0] = (len(relays), 3 * rows)
        relays.append(bulks[k])
    if ctx_size > 1:
        joined = jnp.concatenate([one[0:rows] for one in packets[1:]], axis=0)
        for k in range(1, users):
            for m in range(1, ctx_size):
                places[k, m] = (len(relays), (m - 1) * rows)
            relays.append(swap(joined, "users", k))
    count = ctx_size * slots
    *packs, mine, own, part, spots = call(
        lambda *refs: sort_kernel(users, ctx_size, held, *refs),
        (shape((2 * held, width)),) * (ctx_size - 1)
        + (shape((slots, 2 * width)), shape((count, width)), shape((count, width)), shape((count, 128), F32)),
        (pltpu.VMEM((ctx_size, width, PAD), F32),),
    )(*packets, *bulks)
    packs = [swap(packs[m - 1], "ctx", m) for m in range(1, ctx_size)]
    sums = call(
        lambda *refs: attend_kernel(users, ctx_size, rows, history, places, *refs),
        (shape((slots, width)),) * ctx_size,
        (pltpu.VMEM((count, width), BF16), pltpu.VMEM((count, width), F32)),
    )(spots, part, own, key_cache[0], value_cache[0], *relays)
    sums = [sums[0]] + [swap(sums[m], "ctx", m) for m in range(1, ctx_size)]
    *parts, residual = call(
        lambda *refs: mix_kernel(users, ctx_size, head_size, held, *refs),
        (shape((slots, width), F32),) + (shape((slots, width)),) * (head_size - 1) + (shape((slots, width)),),
    )(owner, mine, out_weight, *sums, *packs)
    got = [parts[0]] + [swap(parts[t], "head", t) for t in range(1, head_size)]
    total = residual.astype(F32)
    for one in got:
        total = total + one.astype(F32)
    slot = lax.broadcasted_iota(jnp.int32, total.shape, 0)
    return jnp.where(slot < counts[0] - lax.axis_index("ctx") * slots, total, 0.0).astype(BF16)[None]


def solution(mesh):
    return jax.shard_map(
        layer,
        mesh=mesh,
        in_specs=(
            P("users"),
            P("users", "ctx", None),
            P("users", "ctx"),
            P(("users", "ctx"), None),
            P(None, None, "head"),
            P("head", None),
            P("users", "ctx", "head"),
            P("users", "ctx", "head"),
        ),
        out_specs=P("users", "ctx", "head"),
        check_vma=False,
    )
```

```python
import jax
import jax.numpy as jnp
from jax import lax
from jax.experimental import pallas as pl
from jax.experimental.pallas import tpu as pltpu
from jax.sharding import PartitionSpec as P


HEAD_DIM = 128
PAD = 16
F32 = jnp.float32
BF16 = jnp.bfloat16


def silu(v):
    return 0.5 * v * (1.0 + jnp.tanh(0.5 * v))


def dot(a, b):
    return jnp.dot(a, b, preferred_element_type=F32)


def vmem():
    return pl.BlockSpec(memory_space=pltpu.VMEM)


def call(kernel, outs, scratch=(), specs=None, far=()):
    given = {} if specs is None else {"in_specs": specs}
    made = pl.pallas_call(
        kernel,
        out_shape=jax.tree.map(lambda o: pltpu.VMEM(o.shape, o.dtype), outs),
        out_specs=jax.tree.map(lambda _: vmem(), outs),
        scratch_shapes=list(scratch),
        compiler_params=pltpu.CompilerParams(vmem_limit_bytes=16 << 20),
        **given,
    )

    def run(*args):
        spaces = [pltpu.HBM if i in far else pltpu.VMEM for i in range(len(args))]
        args = [pltpu.with_memory_space_constraint(x, space) for x, space in zip(args, spaces)]
        return made(*args)

    return run


def shape(dims, kind=BF16):
    return jax.ShapeDtypeStruct(dims, kind)


def normed_of(table_ref):
    x = table_ref[...].astype(F32)
    center = x - jnp.mean(x, axis=1, keepdims=True)
    return (center * lax.rsqrt(jnp.mean(center * center, axis=1, keepdims=True) + 1e-05)).astype(BF16)


def project_kernel(owner_ref, row_ref, table_hbm, weight_hbm, packet_ref, bulk_ref, weight_ref, table_ref, sems):
    rows, model = table_ref.shape
    kinds, width = weight_ref.shape[1:]
    slots = owner_ref.shape[1]
    lanes = 128 * kinds
    half = model // 2
    first_copy = pltpu.make_async_copy(table_hbm, table_ref, sems.at[0])
    first_copy.start()
    copies = [
        pltpu.make_async_copy(weight_hbm.at[at : at + half], weight_ref.at[at : at + half], sems.at[1 + at // half])
        for at in (0, half)
    ]
    for one in copies:
        one.start()
    packet_ref[rows:, 0:slots] = jnp.broadcast_to(owner_ref[...].astype(F32), (PAD, slots)).astype(BF16)
    packet_ref[rows:, slots : 2 * slots] = jnp.broadcast_to(row_ref[...].astype(F32), (PAD, slots)).astype(BF16)
    spread = (
        lax.broadcasted_iota(jnp.int32, (128, lanes), 1) // kinds
        == lax.broadcasted_iota(jnp.int32, (128, lanes), 0)
    ).astype(F32).astype(BF16)
    kind = lax.broadcasted_iota(jnp.int32, (rows, lanes), 1) % kinds
    masks = [(kind == k).astype(F32).astype(BF16) for k in range(kinds)]
    first_copy.wait()
    normed = normed_of(table_ref)
    start = pl.multiple_of(lax.axis_index("head") * width, width)
    bulk_ref[:, 2 * width :] = table_ref[:, pl.ds(start, width)]
    parts = []
    for at in range(0, model, 128):
        wide = dot(normed[:, at : at + 128], spread).astype(BF16)
        parts.append(jnp.concatenate([wide * mask for mask in masks], axis=0))
    for one in copies:
        one.wait()
    total = dot(jnp.concatenate(parts, axis=1), weight_ref[...].reshape(model * kinds, width))
    gates, values, queries, keys = [silu(total[k * rows : (k + 1) * rows]).astype(BF16) for k in range(kinds)]
    packet_ref[0:rows, :] = queries
    bulk_ref[:, width : 2 * width] = gates
    product = queries.astype(F32) * keys.astype(F32)
    for first in range(0, width, HEAD_DIM):
        cols = slice(first, first + HEAD_DIM)
        score = jnp.sum(product[:, cols], axis=1, keepdims=True)
        bulk_ref[:, cols] = (silu(score * HEAD_DIM ** (-0.5)) * values[:, cols].astype(F32)).astype(BF16)


def one_hot(spot, size):
    lanes = lax.broadcasted_iota(jnp.int32, (spot.shape[0], size), 1).astype(F32)
    return (lanes == spot).astype(F32).astype(BF16)


def loop(size, body):
    if size <= 4:
        for j in range(size):
            body(j)
    else:
        lax.fori_loop(0, size, lambda j, c: (body(j), c)[1], 0)


def sort_kernel(users, ctx_size, held, *refs):
    packets, joined_ref, bulks = refs[:ctx_size], refs[ctx_size], refs[ctx_size + 1 : ctx_size + 1 + users]
    outs = refs[ctx_size + 1 + users :]
    sends = outs[: ctx_size - 1]
    extra_ref, query_ref, spot_ref, id_ref = outs[ctx_size - 1 :]
    me_user = lax.axis_index("users")
    me_ctx = lax.axis_index("ctx")
    rows = bulks[0].shape[0]
    count, width = query_ref.shape
    slots = count // ctx_size
    owners = [
        [((me_user ^ k) * ctx_size + (me_ctx ^ m)).astype(F32) for m in range(ctx_size)] for k in range(users)
    ]
    for m in range(ctx_size):
        id_ref[m] = jnp.transpose(packets[m][rows:, :].astype(F32))
    lane = lax.broadcasted_iota(jnp.int32, (slots, 128), 1)

    def find(j):
        owner = id_ref[j, 0:slots, 0:1]
        row = id_ref[j, slots : 2 * slots, 0:1]
        spots = jnp.full((slots, 128), -1.0, F32)
        group = jnp.full((slots, 1), -1.0, F32)
        for k in range(users):
            spot = jnp.full((slots, 1), -1.0, F32)
            for m in range(ctx_size):
                spot = jnp.where(owner == owners[k][m], row + float(m * rows), spot)
            spots = jnp.where(lane == k, spot, spots)
            group = jnp.where(owner == owners[k][0], row + float(k * rows), group)
        first = j * slots if isinstance(j, int) else pl.multiple_of(j * slots, slots)
        spot_ref[pl.ds(first, slots), :] = jnp.where(lane == users, group, spots)

    loop(ctx_size, find)
    block = min(count, 512)
    both = jnp.concatenate([bulk[...] for bulk in bulks], axis=0)

    def gather(b):
        first = b * block if isinstance(b, int) else pl.multiple_of(b * block, block)
        group = spot_ref[pl.ds(first, block), users : users + 1]
        extra_ref[pl.ds(first, block), :] = dot(one_hot(group, users * rows), both).astype(BF16)
        spot = spot_ref[pl.ds(first, block), 0:1]
        query_ref[pl.ds(first, block), :] = dot(one_hot(spot, ctx_size * rows), joined_ref[...]).astype(BF16)

    loop(count // block, gather)
    before = (
        lax.broadcasted_iota(jnp.int32, (slots, slots), 0) < lax.broadcasted_iota(jnp.int32, (slots, slots), 1)
    ).astype(F32).astype(BF16)
    for j in range(1, ctx_size):
        line = packets[j][rows:, 0:slots].astype(F32)
        inside = jnp.zeros(line.shape, jnp.bool_)
        for k in range(users):
            inside = inside | (line == owners[k][0])
        rank = jnp.where(inside, dot(inside.astype(F32).astype(BF16), before), -1.0)[0:1, :]
        keep = lax.broadcasted_iota(jnp.int32, (held, slots), 0).astype(F32) == rank
        sends[j - 1][...] = dot(
            keep.astype(F32).astype(BF16), extra_ref[j * slots : (j + 1) * slots, width:]
        ).astype(BF16)


def attend_kernel(users, ctx_size, history, *refs):
    spot_ref, part_ref, extra_ref, key_ref, value_ref = refs[:5]
    relays = refs[5 : 4 + users]
    outs, sum_ref = refs[4 + users : -1], refs[-1]
    count, width = part_ref.shape
    slots = count // ctx_size
    block = min(count, 512)

    def attend(b):
        first = b * block if isinstance(b, int) else pl.multiple_of(b * block, block)
        queries = part_ref[pl.ds(first, block), :].astype(F32)
        for k in range(1, users):
            spot = spot_ref[pl.ds(first, block), k : k + 1]
            queries = queries + dot(one_hot(spot, relays[k - 1].shape[0]), relays[k - 1][...])
        queries = queries.astype(BF16)
        for at in range(0, width, HEAD_DIM):
            cols = slice(at, at + HEAD_DIM)
            scores = lax.dot_general(
                queries[:, cols], key_ref[:, cols], (((1,), (1,)), ((), ())), preferred_element_type=F32
            ) * (0.5 * HEAD_DIM ** (-0.5))
            weights = (scores + scores * jnp.tanh(scores)).astype(BF16)
            sum_ref[pl.ds(first, block), cols] = dot(weights, value_ref[:, cols])

    loop(count // block, attend)
    for j in range(ctx_size):
        span = slice(j * slots, (j + 1) * slots)
        outs[j][...] = (sum_ref[span, :] * history ** (-0.5) + extra_ref[span, 0:width].astype(F32)).astype(BF16)


def mix_kernel(users, ctx_size, head_size, held, *refs):
    owner_ref, extra_ref, weight_ref = refs[:3]
    sums = refs[3 : 3 + ctx_size]
    packs = refs[3 + ctx_size : 2 + 2 * ctx_size]
    outs = refs[2 + 2 * ctx_size : 2 + 2 * ctx_size + head_size]
    residual_ref = refs[2 + 2 * ctx_size + head_size]
    me_user = lax.axis_index("users")
    me_ctx = lax.axis_index("ctx")
    me_head = lax.axis_index("head")
    slots, width = residual_ref.shape
    owner = jnp.transpose(jnp.broadcast_to(owner_ref[...].astype(F32), (8, slots)))[:, 0:1]
    lanes = 128
    lane = lax.broadcasted_iota(jnp.int32, (slots, lanes), 1)
    inside = jnp.zeros((slots, lanes), jnp.bool_)
    for k in range(users):
        named = (me_user ^ k) * ctx_size + (me_ctx ^ lane)
        inside = inside | ((owner == named.astype(F32)) & (lane < ctx_size))
    after = (
        lax.broadcasted_iota(jnp.int32, (slots, slots), 1) < lax.broadcasted_iota(jnp.int32, (slots, slots), 0)
    ).astype(F32).astype(BF16)
    rank = jnp.where(inside, dot(after, inside.astype(F32).astype(BF16)), -1.0)
    attended = sums[0][...].astype(F32)
    for m in range(1, ctx_size):
        attended = attended + sums[m][...].astype(F32)
    both = extra_ref[0:slots, width:].astype(F32)
    if ctx_size > 1:
        spots = lax.broadcasted_iota(jnp.int32, (slots, (ctx_size - 1) * held), 1).astype(F32)
        spot = jnp.full((slots, 1), -1.0, F32)
        for m in range(1, ctx_size):
            mine = rank[:, m : m + 1]
            spot = jnp.where(mine >= 0.0, mine + float((m - 1) * held), spot)
        both = both + dot(
            (spots == spot).astype(F32).astype(BF16), jnp.concatenate([pack[...] for pack in packs], axis=0)
        )
    gates, residual = both[:, 0:width], both[:, width:]
    residual_ref[...] = residual.astype(BF16)
    parts = []
    for at in range(0, width, HEAD_DIM):
        one = attended[:, at : at + HEAD_DIM]
        center = one - jnp.mean(one, axis=1, keepdims=True)
        parts.append(
            center
            * lax.rsqrt(jnp.mean(center * center, axis=1, keepdims=True) + 1e-05)
            * gates[:, at : at + HEAD_DIM]
        )
    hidden = jnp.concatenate(parts, axis=1).astype(BF16)
    for t in range(head_size):
        first = pl.multiple_of((me_head ^ t) * width, width)
        outs[t][...] = dot(hidden, weight_ref[:, pl.ds(first, width)]).astype(outs[t].dtype)


def swap(x, axis, k):
    return lax.ppermute(x, axis, [(i, i ^ k) for i in range(lax.axis_size(axis))])


def layer(
    counts, cand_owner, cand_row, item_table, proj_weight, out_weight, key_cache, value_cache
):
    users = lax.axis_size("users")
    ctx_size = lax.axis_size("ctx")
    head_size = lax.axis_size("head")
    slots = cand_row.shape[1]
    rows, model = item_table.shape
    width = proj_weight.shape[2]
    span = rows + PAD
    history = key_cache.shape[1] * ctx_size
    capacity = max(2, 2 * slots // (users * ctx_size))
    held = max(PAD, -(-users * min(capacity, slots) // PAD) * PAD)
    owner = cand_owner.reshape(1, slots)
    kinds = proj_weight.shape[1]
    hbm = pl.BlockSpec(memory_space=pl.ANY)
    packet, bulk = call(
        project_kernel,
        (shape((span, width)), shape((rows, 3 * width))),
        (
            pltpu.VMEM((model, kinds, width), BF16),
            pltpu.VMEM((rows, model), BF16),
            pltpu.SemaphoreType.DMA((3,)),
        ),
        specs=[vmem()] * 2 + [hbm] * 2,
        far=(0, 1, 2, 3),
    )(owner, cand_row, item_table, proj_weight)
    packets = [packet] + [swap(packet, "ctx", m) for m in range(1, ctx_size)]
    bulks = [bulk] + [swap(bulk, "users", k) for k in range(1, users)]
    joined = jnp.concatenate([one[0:rows] for one in packets], axis=0)
    relays = [swap(joined, "users", k) for k in range(1, users)]
    count = ctx_size * slots
    *packs, extra, part, spots = call(
        lambda *refs: sort_kernel(users, ctx_size, held, *refs),
        (shape((held, 2 * width)),) * (ctx_size - 1)
        + (shape((count, 3 * width)), shape((count, width)), shape((count, 128), F32)),
        (pltpu.VMEM((ctx_size, width, PAD), F32),),
    )(*packets, joined, *bulks)
    packs = [swap(packs[m - 1], "ctx", m) for m in range(1, ctx_size)]
    sums = call(
        lambda *refs: attend_kernel(users, ctx_size, history, *refs),
        (shape((slots, width)),) * ctx_size,
        (pltpu.VMEM((count, width), F32),),
    )(spots, part, extra, key_cache[0], value_cache[0], *relays)
    sums = [sums[0]] + [swap(sums[m], "ctx", m) for m in range(1, ctx_size)]
    *parts, residual = call(
        lambda *refs: mix_kernel(users, ctx_size, head_size, held, *refs),
        (shape((slots, width), F32),) + (shape((slots, width)),) * (head_size - 1) + (shape((slots, width)),),
    )(owner, extra, out_weight, *sums, *packs)
    got = [parts[0]] + [swap(parts[t], "head", t) for t in range(1, head_size)]
    total = residual.astype(F32)
    for one in got:
        total = total + one.astype(F32)
    slot = lax.broadcasted_iota(jnp.int32, total.shape, 0)
    return jnp.where(slot < counts[0] - lax.axis_index("ctx") * slots, total, 0.0).astype(BF16)[None]


def solution(mesh):
    return jax.shard_map(
        layer,
        mesh=mesh,
        in_specs=(
            P("users"),
            P("users", "ctx", None),
            P("users", "ctx"),
            P(("users", "ctx"), None),
            P(None, None, "head"),
            P("head", None),
            P("users", "ctx", "head"),
            P("users", "ctx", "head"),
        ),
        out_specs=P("users", "ctx", "head"),
        check_vma=False,
    )
```

```python
import jax
import jax.numpy as jnp
from jax import lax
from jax.experimental import pallas as pl
from jax.experimental.pallas import tpu as pltpu
from jax.sharding import PartitionSpec as P


HEAD_DIM = 128
PAD = 16
F32 = jnp.float32
BF16 = jnp.bfloat16


def silu(v):
    return 0.5 * v * (1.0 + jnp.tanh(0.5 * v))


def dot(a, b):
    return jnp.dot(a, b, preferred_element_type=F32)


def vmem():
    return pl.BlockSpec(memory_space=pltpu.VMEM)


def call(kernel, outs, scratch=(), specs=None, far=()):
    given = {} if specs is None else {"in_specs": specs}
    made = pl.pallas_call(
        kernel,
        out_shape=jax.tree.map(lambda o: pltpu.VMEM(o.shape, o.dtype), outs),
        out_specs=jax.tree.map(lambda _: vmem(), outs),
        scratch_shapes=list(scratch),
        compiler_params=pltpu.CompilerParams(vmem_limit_bytes=16 << 20),
        **given,
    )

    def run(*args):
        spaces = [pltpu.HBM if i in far else pltpu.VMEM for i in range(len(args))]
        args = [pltpu.with_memory_space_constraint(x, space) for x, space in zip(args, spaces)]
        return made(*args)

    return run


def shape(dims, kind=BF16):
    return jax.ShapeDtypeStruct(dims, kind)


def normed_of(table_ref):
    x = table_ref[...].astype(F32)
    center = x - jnp.mean(x, axis=1, keepdims=True)
    return (center * lax.rsqrt(jnp.mean(center * center, axis=1, keepdims=True) + 1e-05)).astype(BF16)


def project_kernel(owner_ref, row_ref, table_hbm, weight_hbm, packet_ref, bulk_ref, weight_ref, table_ref, sems):
    rows, model = table_ref.shape
    kinds, width = weight_ref.shape[1:]
    slots = owner_ref.shape[1]
    lanes = 128 * kinds
    half = model // 2
    first_copy = pltpu.make_async_copy(table_hbm, table_ref, sems.at[0])
    first_copy.start()
    copies = [
        pltpu.make_async_copy(weight_hbm.at[at : at + half], weight_ref.at[at : at + half], sems.at[1 + at // half])
        for at in (0, half)
    ]
    for one in copies:
        one.start()
    packet_ref[rows:, 0:slots] = jnp.broadcast_to(owner_ref[...].astype(F32), (PAD, slots)).astype(BF16)
    packet_ref[rows:, slots : 2 * slots] = jnp.broadcast_to(row_ref[...].astype(F32), (PAD, slots)).astype(BF16)
    spread = (
        lax.broadcasted_iota(jnp.int32, (128, lanes), 1) // kinds
        == lax.broadcasted_iota(jnp.int32, (128, lanes), 0)
    ).astype(F32).astype(BF16)
    kind = lax.broadcasted_iota(jnp.int32, (rows, lanes), 1) % kinds
    masks = [(kind == k).astype(F32).astype(BF16) for k in range(kinds)]
    first_copy.wait()
    normed = normed_of(table_ref)
    start = pl.multiple_of(lax.axis_index("head") * width, width)
    bulk_ref[:, 2 * width :] = table_ref[:, pl.ds(start, width)]
    parts = []
    for at in range(0, model, 128):
        wide = dot(normed[:, at : at + 128], spread).astype(BF16)
        parts.append(jnp.concatenate([wide * mask for mask in masks], axis=0))
    for one in copies:
        one.wait()
    total = dot(jnp.concatenate(parts, axis=1), weight_ref[...].reshape(model * kinds, width))
    gates, values, queries, keys = [silu(total[k * rows : (k + 1) * rows]).astype(BF16) for k in range(kinds)]
    packet_ref[0:rows, :] = queries
    bulk_ref[:, width : 2 * width] = gates
    product = queries.astype(F32) * keys.astype(F32)
    for first in range(0, width, HEAD_DIM):
        cols = slice(first, first + HEAD_DIM)
        score = jnp.sum(product[:, cols], axis=1, keepdims=True)
        bulk_ref[:, cols] = (silu(score * HEAD_DIM ** (-0.5)) * values[:, cols].astype(F32)).astype(BF16)


def one_hot(spot, size):
    lanes = lax.broadcasted_iota(jnp.int32, (spot.shape[0], size), 1).astype(F32)
    return (lanes == spot).astype(F32).astype(BF16)


def loop(size, body):
    if size <= 4:
        for j in range(size):
            body(j)
    else:
        lax.fori_loop(0, size, lambda j, c: (body(j), c)[1], 0)


def sort_kernel(users, ctx_size, held, *refs):
    packets, joined_ref, bulks = refs[:ctx_size], refs[ctx_size], refs[ctx_size + 1 : ctx_size + 1 + users]
    outs = refs[ctx_size + 1 + users :]
    sends = outs[: ctx_size - 1]
    extra_ref, query_ref, spot_ref, id_ref = outs[ctx_size - 1 :]
    me_user = lax.axis_index("users")
    me_ctx = lax.axis_index("ctx")
    rows = bulks[0].shape[0]
    count, width = query_ref.shape
    slots = count // ctx_size
    owners = [
        [((me_user ^ k) * ctx_size + (me_ctx ^ m)).astype(F32) for m in range(ctx_size)] for k in range(users)
    ]
    for m in range(ctx_size):
        id_ref[m] = jnp.transpose(packets[m][rows:, :].astype(F32))
    lane = lax.broadcasted_iota(jnp.int32, (slots, 128), 1)

    def find(j):
        owner = id_ref[j, 0:slots, 0:1]
        row = id_ref[j, slots : 2 * slots, 0:1]
        spots = jnp.full((slots, 128), -1.0, F32)
        group = jnp.full((slots, 1), -1.0, F32)
        for k in range(users):
            spot = jnp.full((slots, 1), -1.0, F32)
            for m in range(ctx_size):
                spot = jnp.where(owner == owners[k][m], row + float(m * rows), spot)
            spots = jnp.where(lane == k, spot, spots)
            group = jnp.where(owner == owners[k][0], row + float(k * rows), group)
        first = j * slots if isinstance(j, int) else pl.multiple_of(j * slots, slots)
        spot_ref[pl.ds(first, slots), :] = jnp.where(lane == users, group, spots)

    loop(ctx_size, find)
    block = min(count, 512)
    both = jnp.concatenate([bulk[...] for bulk in bulks], axis=0)

    def gather(b):
        first = b * block if isinstance(b, int) else pl.multiple_of(b * block, block)
        group = spot_ref[pl.ds(first, block), users : users + 1]
        extra_ref[pl.ds(first, block), :] = dot(one_hot(group, users * rows), both).astype(BF16)
        spot = spot_ref[pl.ds(first, block), 0:1]
        query_ref[pl.ds(first, block), :] = dot(one_hot(spot, ctx_size * rows), joined_ref[...]).astype(BF16)

    loop(count // block, gather)
    before = (
        lax.broadcasted_iota(jnp.int32, (slots, slots), 0) < lax.broadcasted_iota(jnp.int32, (slots, slots), 1)
    ).astype(F32).astype(BF16)
    for j in range(1, ctx_size):
        line = packets[j][rows:, 0:slots].astype(F32)
        inside = jnp.zeros(line.shape, jnp.bool_)
        for k in range(users):
            inside = inside | (line == owners[k][0])
        rank = jnp.where(inside, dot(inside.astype(F32).astype(BF16), before), -1.0)[0:1, :]
        keep = lax.broadcasted_iota(jnp.int32, (held, slots), 0).astype(F32) == rank
        sends[j - 1][...] = dot(
            keep.astype(F32).astype(BF16), extra_ref[j * slots : (j + 1) * slots, width:]
        ).astype(BF16)


def attend_kernel(users, ctx_size, history, *refs):
    spot_ref, part_ref, extra_ref, key_ref, value_ref = refs[:5]
    relays = refs[5 : 4 + users]
    outs, sum_ref = refs[4 + users : -1], refs[-1]
    count, width = part_ref.shape
    slots = count // ctx_size
    block = min(count, 512)

    def attend(b):
        first = b * block if isinstance(b, int) else pl.multiple_of(b * block, block)
        queries = part_ref[pl.ds(first, block), :].astype(F32)
        for k in range(1, users):
            spot = spot_ref[pl.ds(first, block), k : k + 1]
            queries = queries + dot(one_hot(spot, relays[k - 1].shape[0]), relays[k - 1][...])
        queries = queries.astype(BF16)
        for at in range(0, width, HEAD_DIM):
            cols = slice(at, at + HEAD_DIM)
            scores = lax.dot_general(
                queries[:, cols], key_ref[:, cols], (((1,), (1,)), ((), ())), preferred_element_type=F32
            ) * (0.5 * HEAD_DIM ** (-0.5))
            weights = (scores + scores * jnp.tanh(scores)).astype(BF16)
            sum_ref[pl.ds(first, block), cols] = dot(weights, value_ref[:, cols])

    loop(count // block, attend)
    for j in range(ctx_size):
        span = slice(j * slots, (j + 1) * slots)
        outs[j][...] = (sum_ref[span, :] * history ** (-0.5) + extra_ref[span, 0:width].astype(F32)).astype(BF16)


def prepare_kernel(users, ctx_size, held, *refs):
    owner_ref, extra_ref = refs[:2]
    packs = refs[2:-2]
    gate_ref, residual_ref = refs[-2:]
    me_user = lax.axis_index("users")
    me_ctx = lax.axis_index("ctx")
    slots, width = residual_ref.shape
    owner = jnp.transpose(jnp.broadcast_to(owner_ref[...].astype(F32), (8, slots)))[:, 0:1]
    lane = lax.broadcasted_iota(jnp.int32, (slots, 128), 1)
    inside = jnp.zeros((slots, 128), jnp.bool_)
    for k in range(users):
        named = (me_user ^ k) * ctx_size + (me_ctx ^ lane)
        inside = inside | ((owner == named.astype(F32)) & (lane < ctx_size))
    after = (
        lax.broadcasted_iota(jnp.int32, (slots, slots), 1) < lax.broadcasted_iota(jnp.int32, (slots, slots), 0)
    ).astype(F32).astype(BF16)
    rank = jnp.where(inside, dot(after, inside.astype(F32).astype(BF16)), -1.0)
    both = extra_ref[0:slots, width:].astype(F32)
    if packs:
        spots = lax.broadcasted_iota(jnp.int32, (slots, len(packs) * held), 1).astype(F32)
        spot = jnp.full((slots, 1), -1.0, F32)
        for m in range(1, ctx_size):
            mine = rank[:, m : m + 1]
            spot = jnp.where(mine >= 0.0, mine + float((m - 1) * held), spot)
        both = both + dot(
            (spots == spot).astype(F32).astype(BF16), jnp.concatenate([pack[...] for pack in packs], axis=0)
        )
    gate_ref[...] = both[:, 0:width]
    residual_ref[...] = both[:, width:].astype(BF16)


def mix_kernel(ctx_size, *refs):
    gate_ref, weight_ref = refs[:2]
    sums = refs[2 : 2 + ctx_size]
    outs = refs[2 + ctx_size :]
    me_head = lax.axis_index("head")
    width = gate_ref.shape[1]
    attended = sums[0][...].astype(F32)
    for one in sums[1:]:
        attended = attended + one[...].astype(F32)
    parts = []
    for at in range(0, width, HEAD_DIM):
        one = attended[:, at : at + HEAD_DIM]
        center = one - jnp.mean(one, axis=1, keepdims=True)
        parts.append(
            center
            * lax.rsqrt(jnp.mean(center * center, axis=1, keepdims=True) + 1e-05)
            * gate_ref[:, at : at + HEAD_DIM]
        )
    hidden = jnp.concatenate(parts, axis=1).astype(BF16)
    for t in range(len(outs)):
        first = pl.multiple_of((me_head ^ t) * width, width)
        outs[t][...] = dot(hidden, weight_ref[:, pl.ds(first, width)]).astype(outs[t].dtype)


def swap(x, axis, k):
    return lax.ppermute(x, axis, [(i, i ^ k) for i in range(lax.axis_size(axis))])


def layer(
    counts, cand_owner, cand_row, item_table, proj_weight, out_weight, key_cache, value_cache
):
    users = lax.axis_size("users")
    ctx_size = lax.axis_size("ctx")
    head_size = lax.axis_size("head")
    slots = cand_row.shape[1]
    rows, model = item_table.shape
    width = proj_weight.shape[2]
    span = rows + PAD
    history = key_cache.shape[1] * ctx_size
    capacity = max(2, 2 * slots // (users * ctx_size))
    held = max(PAD, -(-users * min(capacity, slots) // PAD) * PAD)
    owner = cand_owner.reshape(1, slots)
    kinds = proj_weight.shape[1]
    hbm = pl.BlockSpec(memory_space=pl.ANY)
    packet, bulk = call(
        project_kernel,
        (shape((span, width)), shape((rows, 3 * width))),
        (
            pltpu.VMEM((model, kinds, width), BF16),
            pltpu.VMEM((rows, model), BF16),
            pltpu.SemaphoreType.DMA((3,)),
        ),
        specs=[vmem()] * 2 + [hbm] * 2,
        far=(0, 1, 2, 3),
    )(owner, cand_row, item_table, proj_weight)
    packets = [packet] + [swap(packet, "ctx", m) for m in range(1, ctx_size)]
    bulks = [bulk] + [swap(bulk, "users", k) for k in range(1, users)]
    joined = jnp.concatenate([one[0:rows] for one in packets], axis=0)
    relays = [swap(joined, "users", k) for k in range(1, users)]
    count = ctx_size * slots
    *packs, extra, part, spots = call(
        lambda *refs: sort_kernel(users, ctx_size, held, *refs),
        (shape((held, 2 * width)),) * (ctx_size - 1)
        + (shape((count, 3 * width)), shape((count, width)), shape((count, 128), F32)),
        (pltpu.VMEM((ctx_size, width, PAD), F32),),
    )(*packets, joined, *bulks)
    packs = [swap(packs[m - 1], "ctx", m) for m in range(1, ctx_size)]
    sums = call(
        lambda *refs: attend_kernel(users, ctx_size, history, *refs),
        (shape((slots, width)),) * ctx_size,
        (pltpu.VMEM((count, width), F32),),
    )(spots, part, extra, key_cache[0], value_cache[0], *relays)
    sums = [sums[0]] + [swap(sums[m], "ctx", m) for m in range(1, ctx_size)]
    gates, residual = call(
        lambda *refs: prepare_kernel(users, ctx_size, held, *refs), (shape((slots, width), F32), shape((slots, width)))
    )(owner, extra, *packs)
    parts = call(
        lambda *refs: mix_kernel(ctx_size, *refs),
        (shape((slots, width), F32),) + (shape((slots, width)),) * (head_size - 1),
    )(gates, out_weight, *sums)
    got = [parts[0]] + [swap(parts[t], "head", t) for t in range(1, head_size)]
    total = residual.astype(F32)
    for one in got:
        total = total + one.astype(F32)
    slot = lax.broadcasted_iota(jnp.int32, total.shape, 0)
    return jnp.where(slot < counts[0] - lax.axis_index("ctx") * slots, total, 0.0).astype(BF16)[None]


def solution(mesh):
    return jax.shard_map(
        layer,
        mesh=mesh,
        in_specs=(
            P("users"),
            P("users", "ctx", None),
            P("users", "ctx"),
            P(("users", "ctx"), None),
            P(None, None, "head"),
            P("head", None),
            P("users", "ctx", "head"),
            P("users", "ctx", "head"),
        ),
        out_specs=P("users", "ctx", "head"),
        check_vma=False,
    )
```
